32 devices in a mesh: tm: 8 (over z, y), opt: 4 (over x, core).
Axes of the slice: x: 2, y: 2, z: 4, core: 2. Of those that a mesh axis runs over, the one named last changes fastest.
Arguments:
- wave: float32 [8, 8, 4160], P('opt', 'tm'), may hold values from -6 to 6
- crop_offsets: int32 [8], P('opt'), may hold values from 0 to 64, as said below
- squeeze_order: int32 [8], replicated, may hold values from 0 to 7, each once
- mel: bfloat16 [8, 128, 80], P('opt', 'tm'), may hold values from -6 to 6
- mel_index: int32 [8, 4096, 8], P('opt', 'tm'), may hold values from 0 to 15, as said below
- soap_slots: int32 [12], replicated, may hold values from 0 to 11, each once
- step_count: int32 [1], replicated, may hold values from 2 to 20
- in_weight: float32 [12, 512, 512], P('opt'), may hold values from -0.15625 to 0.15625
- soap_first: float32 [12, 512, 512], P('opt'), may hold values from -9.1552734e-05 to 9.1552734e-05
- soap_second: float32 [12, 512, 512], P('opt'), may hold values from 1.5258789e-09 to 2.4414062e-08
- left_stats: float32 [12, 512, 512], P('opt'), as said below
- right_stats: float32 [12, 512, 512], P('opt'), as said below
- left_basis: float32 [12, 512, 512], P('opt')
- right_basis: float32 [12, 512, 512], P('opt')
- cond_weight: float32 [2048, 640], P('tm', 'opt'), may hold values from -0.25 to 0.25
- cond_first: float32 [2048, 640], P('tm', 'opt'), may hold values from -9.1552734e-05 to 9.1552734e-05
- cond_second: float32 [2048, 640], P('tm', 'opt'), may hold values from 1.5258789e-09 to 2.4414062e-08
- out_weight: float32 [3, 512, 512], P(None, 'tm', 'opt'), may hold values from -0.25 to 0.25
- out_first: float32 [3, 512, 512], P(None, 'tm', 'opt'), may hold values from -9.1552734e-05 to 9.1552734e-05
- out_second: float32 [3, 512, 512], P(None, 'tm', 'opt'), may hold values from 1.5258789e-09 to 2.4414062e-08
- aux_params: float32 [17, 512], replicated
- aux_first: float32 [17, 512], replicated
- aux_second: float32 [17, 512], replicated
- flow_params: float32 [6, 7], replicated
- flow_first: float32 [6, 7], replicated, may hold values from -0.15625 to 0.15625
- flow_second: float32 [6, 7], replicated, may hold values from 1e-05 to 0.001
Outputs:
- loss: float32 [], replicated
- in_new: float32 [12, 512, 512], P('opt')
- soap_first_new: float32 [12, 512, 512], P('opt')
- soap_second_new: float32 [12, 512, 512], P('opt')
- left_stats_new: float32 [12, 512, 512], P('opt')
- right_stats_new: float32 [12, 512, 512], P('opt')
- left_basis_new: float32 [12, 512, 512], P('opt')
- right_basis_new: float32 [12, 512, 512], P('opt')
- cond_new: float32 [2048, 640], P('tm', 'opt')
- cond_first_new: float32 [2048, 640], P('tm', 'opt')
- cond_second_new: float32 [2048, 640], P('tm', 'opt')
- out_new: float32 [3, 512, 512], P(None, 'tm', 'opt')
- out_first_new: float32 [3, 512, 512], P(None, 'tm', 'opt')
- out_second_new: float32 [3, 512, 512], P(None, 'tm', 'opt')
- aux_new: float32 [17, 512], replicated
- aux_first_new: float32 [17, 512], replicated
- aux_second_new: float32 [17, 512], replicated
- flow_new: float32 [6, 7], replicated
- flow_first_new: float32 [6, 7], replicated
- flow_second_new: float32 [6, 7], replicated
The draws below stay inside these ranges and needn't reach their ends.
Inputs may be any that keep to these rules, and one draw needn't show every extreme that they name: `crop_offsets`: 0 and 64 both occur. `mel_index`: counted within the 16 frames of the same block of 512 groups. `soap_slots`: each slot number once. `squeeze_order`: each sample once. `left_stats`: symmetric positive definite. `right_stats`: symmetric positive definite.
All inputs are finite; a program needn't handle non-finite values.
Results may differ from the reference program's by a relative error of at most 0.0065.
Values may be sent and summed in bfloat16 or wider, within the bound.
No kernel may reach another device: no remote copies, remote signals or barrier semaphores. Data moves between devices by JAX's collectives and lax.ppermute only.
A program may use at most 192 MiB of HBM per device.

```python
import math
import jax
import jax.numpy as jnp
from jax import lax

H = 512
MEL = 80
LAYERS = 2
FIRST_DILATION = 64
HOP = 256
SHIFT_MAX = 64
G_DEV = 512
CROPS = 8
GROUPS = 4096
TOKENS = 32768
FR_DEV = 16
FRAMES = 128
SLAB = 4160
NMAT = 12
AUX = 17
N_TM = 8


def draw_crop_offsets(key, part):
    values = jax.random.randint(key, (CROPS,), 0, SHIFT_MAX + 1)
    picked = jax.random.randint(jax.random.fold_in(key, 7), (), 0, CROPS)
    places = jnp.arange(CROPS)
    values = jnp.where(places == picked, SHIFT_MAX, values)
    return jnp.where(places == (picked + 1) % CROPS, 0, values).astype(jnp.int32)


def draw_mel_index(key, part):
    groups_local = jnp.arange(GROUPS) % G_DEV
    sample = 8 * groups_local[:, None] + jnp.arange(8)[None, :]
    jitter = jax.random.randint(key, (CROPS, GROUPS, 8), -1, 2)
    return jnp.clip(sample[None] // HOP + jitter, 0, FR_DEV - 1).astype(jnp.int32)


def stats_draw(key, salt):
    folded = jax.random.fold_in(key, salt)
    random_part = jax.random.normal(folded, (NMAT, H, H), jnp.float32)
    diagonal = jax.random.uniform(jax.random.fold_in(folded, 1), (NMAT, H), jnp.float32, 2.5, 3.5)
    symmetric = (random_part + jnp.swapaxes(random_part, 1, 2)) * (0.5 / H ** 0.5)
    magnitude = 2.5e-05 * H
    return magnitude * (symmetric + diagonal[:, :, None] * jnp.eye(H, dtype=jnp.float32))


def basis_draw(key, salt):
    folded = jax.random.fold_in(key, salt)
    random_part = jax.random.normal(folded, (NMAT, H, H), jnp.float32)
    return jnp.eye(H, dtype=jnp.float32) + random_part * (0.3 / H ** 0.5)


def draw_left_stats(key, part):
    return stats_draw(key, 11)


def draw_right_stats(key, part):
    return stats_draw(key, 12)


def draw_left_basis(key, part):
    return basis_draw(key, 13)


def draw_right_basis(key, part):
    return basis_draw(key, 14)


def draw_aux_params(key, part):
    random_part = jax.random.normal(key, (AUX, H), jnp.float32)
    row_index = jnp.arange(AUX)[:, None]
    magnitude = jnp.where(row_index < 3, 0.5, jnp.where(row_index < 4 + 2 * LAYERS, 0.2, jnp.where(row_index < 3 + 4 * LAYERS, 0.1, 0.5 / H ** 0.5)))
    return random_part * magnitude


def aux_rows_scale():
    row_index = jnp.arange(AUX)[:, None]
    root_width = H ** 0.5
    row_scale = jnp.where(row_index < 3, 0.045 / root_width, 0.14 / root_width)
    gate_rows = (row_index >= 4) & (row_index < 4 + 2 * LAYERS)
    row_scale = jnp.where(gate_rows, jnp.where((row_index - 4) % 2 == 0, 0.1 / root_width, 0.034 / root_width), row_scale)
    row_scale = jnp.where((row_index >= 4 + 2 * LAYERS) & (row_index < 3 + 3 * LAYERS), 0.1 / root_width, row_scale)
    row_scale = jnp.where((row_index >= 3 + 3 * LAYERS) & (row_index < 4 * LAYERS + 3), 0.58 / root_width, row_scale)
    row_scale = jnp.where(row_index >= 4 * LAYERS + 3, jnp.where(row_index < 4 * LAYERS + 6, 0.09, 0.01), row_scale)
    return row_scale * jnp.ones((AUX, H), jnp.float32)


def draw_aux_first(key, part):
    row_scale = aux_rows_scale()
    random_part = jax.random.normal(key, (AUX, H), jnp.float32)
    return 0.12 * row_scale * random_part


def draw_aux_second(key, part):
    row_scale = aux_rows_scale()
    spread_factor = jnp.exp(jax.random.uniform(key, (AUX, H), jnp.float32, 0.0, 1.3862944))
    return 0.0101 * row_scale * row_scale * spread_factor


def draw_flow_params(key, part):
    diagonal = jax.random.uniform(key, (6,), jnp.float32, 1.5, 2.5)
    spread = jax.random.uniform(jax.random.fold_in(key, 3), (6, 6), jnp.float32, -0.25, 0.25)
    matrix = jnp.where(jnp.eye(6, dtype=bool), diagonal[:, None], spread)
    biases = 0.3 * jax.random.normal(jax.random.fold_in(key, 5), (6, 1), jnp.float32)
    return jnp.concatenate([matrix, biases], axis=1)


def level_of(stream_key, shape, split, least, high):
    def one(position, parts):
        draws = jax.random.uniform(jax.random.fold_in(jax.random.fold_in(stream_key, 6), position), (parts,), jnp.float32, least / len(split), high / len(split))
        return jnp.repeat(jnp.exp(draws), shape[position] // parts).reshape((-1,) + (1,) * (len(shape) - position - 1))

    factor_of = one(*split[0])
    for cut in split[1:]:
        factor_of = factor_of * one(*cut)
    return factor_of


def gaussian(stream_key, dims, scale, bound, pieces=(), held_as=jnp.bfloat16):
    result = jax.random.normal(stream_key, dims, jnp.float32) * scale
    if len(pieces) > 0:
        result = level_of(stream_key, dims, pieces, -0.22, 0.18) * result
    return jnp.clip(result, min=-bound, max=bound).astype(held_as)


def setup_inputs(seed: int = 0) -> dict:
    streams_of = jax.random.split(jax.random.key(seed), 27)
    wave = gaussian(streams_of[0], (CROPS, N_TM, SLAB), 1.0, 6.0, ((0, 4), (1, 8)), jnp.float32)
    crop_offsets = draw_crop_offsets(jax.random.fold_in(streams_of[26], 71), 0)
    squeeze_order = jax.random.permutation(streams_of[2], 8).astype(jnp.int32)
    mel = gaussian(streams_of[3], (CROPS, FRAMES, MEL), 1.0, 6.0, ((0, 4), (1, 8)))
    mel_index = draw_mel_index(jax.random.fold_in(streams_of[26], 71), 0)
    soap_slots = jax.random.permutation(streams_of[5], NMAT).astype(jnp.int32)
    step_count = jax.random.randint(streams_of[6], (1,), 2, 21).astype(jnp.int32)
    in_weight = gaussian(streams_of[7], (NMAT, H, H), (3 * H) ** -0.5, 0.15625, ((0, 4),), jnp.float32)
    soap_first = gaussian(streams_of[8], (NMAT, H, H), (0.0011 / TOKENS ** 0.5), 9.1552734375e-05, ((0, 4),), jnp.float32)
    soap_second = jnp.clip(jnp.exp(math.log(2.4414061883248905e-08) - 2.7725887 * jax.random.uniform(streams_of[9], (NMAT, H, H), jnp.float32) ** level_of(streams_of[9], (NMAT, H, H), ((0, 4),), -0.2, 0.2)), 1.5258788677030566e-09, 2.4414061883248905e-08)
    left_stats = draw_left_stats(jax.random.fold_in(streams_of[26], 71), 0)
    right_stats = draw_right_stats(jax.random.fold_in(streams_of[26], 71), 0)
    left_basis = draw_left_basis(jax.random.fold_in(streams_of[26], 71), 0)
    right_basis = draw_right_basis(jax.random.fold_in(streams_of[26], 71), 0)
    cond_weight = gaussian(streams_of[14], (2 * H * LAYERS, 8 * MEL), (8 * MEL) ** -0.5, 0.25, ((0, 8), (1, 4)), jnp.float32)
    cond_first = gaussian(streams_of[15], (2 * H * LAYERS, 8 * MEL), (0.0011 / TOKENS ** 0.5), 9.1552734375e-05, ((0, 8), (1, 4)), jnp.float32)
    cond_second = jnp.clip(jnp.exp(math.log(2.4414061883248905e-08) - 2.7725887 * jax.random.uniform(streams_of[16], (2 * H * LAYERS, 8 * MEL), jnp.float32) ** level_of(streams_of[16], (2 * H * LAYERS, 8 * MEL), ((0, 8), (1, 4)), -0.2, 0.2)), 1.5258788677030566e-09, 2.4414061883248905e-08)
    out_weight = gaussian(streams_of[17], (2 * LAYERS - 1, H, H), H ** -0.5, 0.25, ((1, 8), (2, 4)), jnp.float32)
    out_first = gaussian(streams_of[18], (2 * LAYERS - 1, H, H), (0.0011 / TOKENS ** 0.5), 9.1552734375e-05, ((1, 8), (2, 4)), jnp.float32)
    out_second = jnp.clip(jnp.exp(math.log(2.4414061883248905e-08) - 2.7725887 * jax.random.uniform(streams_of[19], (2 * LAYERS - 1, H, H), jnp.float32) ** level_of(streams_of[19], (2 * LAYERS - 1, H, H), ((1, 8), (2, 4)), -0.2, 0.2)), 1.5258788677030566e-09, 2.4414061883248905e-08)
    aux_params = draw_aux_params(jax.random.fold_in(streams_of[26], 71), 0)
    aux_first = draw_aux_first(jax.random.fold_in(streams_of[26], 71), 0)
    aux_second = draw_aux_second(jax.random.fold_in(streams_of[26], 71), 0)
    flow_params = draw_flow_params(jax.random.fold_in(streams_of[26], 71), 0)
    flow_first = gaussian(streams_of[24], (6, 7), 0.01, 0.15625, (), jnp.float32)
    flow_second = jnp.clip(jnp.exp(jax.random.uniform(streams_of[25], (6, 7), jnp.float32, math.log(9.999999747378752e-06), math.log(0.001))), 9.999999747378752e-06, 0.001)
    return {"wave": wave, "crop_offsets": crop_offsets, "squeeze_order": squeeze_order, "mel": mel, "mel_index": mel_index, "soap_slots": soap_slots, "step_count": step_count, "in_weight": in_weight, "soap_first": soap_first, "soap_second": soap_second, "left_stats": left_stats, "right_stats": right_stats, "left_basis": left_basis, "right_basis": right_basis, "cond_weight": cond_weight, "cond_first": cond_first, "cond_second": cond_second, "out_weight": out_weight, "out_first": out_first, "out_second": out_second, "aux_params": aux_params, "aux_first": aux_first, "aux_second": aux_second, "flow_params": flow_params, "flow_first": flow_first, "flow_second": flow_second}


highest = lax.Precision.HIGHEST
beta_first = 0.9
beta_second = 0.99
beta_stats = 0.95
learn_rate = 0.02
aux_rate = 0.15
epsilon = 1e-08
decay_weight = 0.01
early_weight = 0.5

@jax.custom_vjp
def low(v):
    return lax.optimization_barrier(v.astype(jnp.bfloat16)).astype(jnp.float32)

@jax.custom_vjp
def low_back(v):
    return v

def low_keep(v):
    return (low(v), None)

def low_pass(kept, grad):
    return (grad,)

def back_keep(v):
    return (v, None)

def back_low(kept, grad):
    return (low(grad),)
low.defvjp(low_keep, low_pass)
low_back.defvjp(back_keep, back_low)

def full_dot(matrix_a, matrix_b):
    return jnp.dot(matrix_a.astype(jnp.float32), matrix_b.astype(jnp.float32), precision=highest, preferred_element_type=jnp.float32)

def orthonormal(matrix):
    factor = jnp.linalg.cholesky(full_dot(matrix.T, matrix))
    return jax.scipy.linalg.solve_triangular(factor, matrix.T, lower=True).T

def soap_update(weight, gradient, moment_one, moment_two, left_stats, right_stats, left_basis, right_basis, steps_done):
    rotated = full_dot(full_dot(left_basis.T, gradient), right_basis)
    moment_one = beta_first * moment_one + (1.0 - beta_first) * rotated
    moment_two = beta_second * moment_two + (1.0 - beta_second) * rotated * rotated
    direction = moment_one / (1.0 - beta_first ** steps_done) / (jnp.sqrt(moment_two / (1.0 - beta_second ** steps_done)) + epsilon)
    weight = weight - learn_rate * (full_dot(full_dot(left_basis, direction), right_basis.T) + decay_weight * weight)
    left_stats = beta_stats * left_stats + (1.0 - beta_stats) * full_dot(gradient, gradient.T)
    right_stats = beta_stats * right_stats + (1.0 - beta_stats) * full_dot(gradient.T, gradient)
    left_new = orthonormal(full_dot(left_stats, left_basis))
    right_new = orthonormal(full_dot(right_stats, right_basis))
    initial = full_dot(full_dot(left_basis, moment_one), right_basis.T)
    moment_one = full_dot(full_dot(left_new.T, initial), right_new)
    return (weight, moment_one, moment_two, left_stats, right_stats, left_new, right_new)

def adamw_update(weight, gradient, moment_one, moment_two, steps_done, rate_value):
    moment_one = beta_first * moment_one + (1.0 - beta_first) * gradient
    moment_two = beta_second * moment_two + (1.0 - beta_second) * gradient * gradient
    direction = moment_one / (1.0 - beta_first ** steps_done) / (jnp.sqrt(moment_two / (1.0 - beta_second ** steps_done)) + epsilon)
    weight = weight - rate_value * (direction + decay_weight * weight)
    return (weight, moment_one, moment_two)

def crop_terms(params, squeezed, conditioning):
    matrices, cond_weight, out_weight, aux_params, flow_params = params
    every_tap_weight = jnp.transpose(low(matrices).reshape(LAYERS, 3, 2, H, H), (0, 1, 3, 2, 4)).reshape(LAYERS, 3, H, 2 * H)
    out_low = low(out_weight)
    spectral = full_dot(conditioning, low(cond_weight).T)
    mixed = full_dot(squeezed[:, 2:], flow_params[:, :6].T)
    lower_half = mixed[:, :3]
    upper_half = mixed[:, 3:]
    hidden_state = full_dot(lower_half, aux_params[0:3]) + aux_params[3]
    skip_total = jnp.zeros((GROUPS, H), jnp.float32)
    bias_base = 4 + 2 * LAYERS
    for layer_number in range(LAYERS):
        dilation_step = FIRST_DILATION * 2 ** layer_number
        padded_input = jnp.pad(low(hidden_state), ((dilation_step, dilation_step), (0, 0)))
        before_gate = spectral[:, 2 * H * layer_number:2 * H * (layer_number + 1)] + aux_params[4 + 2 * layer_number:6 + 2 * layer_number].reshape(2 * H)
        for k in range(3):
            before_gate = before_gate + full_dot(padded_input[k * dilation_step:k * dilation_step + GROUPS], every_tap_weight[layer_number, k])
        before_gate = low_back(before_gate)
        gated = low(jnp.tanh(before_gate[:, :H]) * jax.nn.sigmoid(before_gate[:, H:]))
        if layer_number < LAYERS - 1:
            hidden_state = hidden_state + low_back(full_dot(gated, out_low[layer_number]) + aux_params[bias_base + layer_number])
        skip_total = skip_total + low_back(full_dot(gated, out_low[LAYERS - 1 + layer_number]) + aux_params[bias_base + LAYERS - 1 + layer_number])
    outputs = full_dot(skip_total, aux_params[4 * LAYERS + 3:].T) + flow_params[:, 6]
    log_scale = outputs[:, :3]
    z_upper = jnp.exp(log_scale) * upper_half + outputs[:, 3:]
    final_part = 0.5 * jnp.sum(lower_half * lower_half) + 0.5 * jnp.sum(z_upper * z_upper) - jnp.sum(log_scale)
    early_part = 0.5 * jnp.sum(squeezed[:, :2] * squeezed[:, :2])
    return jnp.stack([final_part, early_part])

def reference(wave, crop_offsets, squeeze_order, mel, mel_index, soap_slots, step_count, in_weight, soap_first, soap_second, left_stats, right_stats, left_basis, right_basis, cond_weight, cond_first, cond_second, out_weight, out_first, out_second, aux_params, aux_first, aux_second, flow_params, flow_first, flow_second):
    inverse = jnp.argsort(soap_slots)

    def squeeze_one(samples, offset):
        segment = lax.dynamic_slice_in_dim(samples, offset, 8 * G_DEV, 1)
        return jnp.take(segment.reshape(GROUPS, 8), squeeze_order, axis=1)
    squeezed = jax.vmap(squeeze_one)(wave, crop_offsets)
    block_start = jnp.arange(GROUPS, dtype=jnp.int32) // G_DEV * FR_DEV
    frame_rows = (mel_index + block_start[None, :, None]).astype(jnp.int32)

    def lookup(frames_table, frame_picks):
        return jnp.take(frames_table, frame_picks.reshape(-1), axis=0).reshape(GROUPS, 8 * MEL)
    conditioning = jax.vmap(lookup)(mel.astype(jnp.float32), frame_rows)
    params = (jnp.take(in_weight, inverse, axis=0), cond_weight, out_weight, aux_params, flow_params)
    scale_final = 1.0 / (6.0 * TOKENS)
    scale_early = early_weight / (2.0 * TOKENS)

    def objective(weights):

        def one_crop(running, crop_items):
            return (running + jax.checkpoint(crop_terms)(weights, crop_items[0], crop_items[1]), None)
        totals, _ = lax.scan(one_crop, jnp.zeros((2,), jnp.float32), (squeezed, conditioning))
        log_det = jnp.linalg.slogdet(weights[4][:, :6])[1]
        return totals[0] * scale_final + totals[1] * scale_early - log_det / 6.0
    loss, pullback = jax.vjp(objective, params)
    gradients = pullback(jnp.ones_like(loss))[0]
    steps_done = step_count[0].astype(jnp.float32)
    grad_slots = jnp.take(gradients[0], soap_slots, axis=0)
    in_new, soap_first_new, soap_second_new, left_stats_new, right_stats_new, left_basis_new, right_basis_new = jax.vmap(soap_update, in_axes=(0, 0, 0, 0, 0, 0, 0, 0, None))(in_weight, grad_slots, soap_first, soap_second, left_stats, right_stats, left_basis, right_basis, steps_done)
    cond_new, cond_first_new, cond_second_new = adamw_update(cond_weight, gradients[1], cond_first, cond_second, steps_done, learn_rate)
    out_new, out_first_new, out_second_new = adamw_update(out_weight, gradients[2], out_first, out_second, steps_done, learn_rate)
    aux_new, aux_first_new, aux_second_new = adamw_update(aux_params, gradients[3], aux_first, aux_second, steps_done, aux_rate)
    flow_new, flow_first_new, flow_second_new = adamw_update(flow_params, gradients[4], flow_first, flow_second, steps_done, learn_rate)
    return (loss, in_new, soap_first_new, soap_second_new, left_stats_new, right_stats_new, left_basis_new, right_basis_new, cond_new, cond_first_new, cond_second_new, out_new, out_first_new, out_second_new, aux_new, aux_first_new, aux_second_new, flow_new, flow_first_new, flow_second_new)
```

```python
import jax
import jax.numpy as jnp
from jax import lax
from jax.experimental import pallas as pl
from jax.experimental.pallas import tpu as pltpu
from jax.sharding import PartitionSpec as P

H = 512
MEL = 80
LAYERS = 2
FIRST_DILATION = 64
G_DEV = 512
FR_DEV = 16
NMAT = 12


highest = lax.Precision.HIGHEST
beta_first = 0.9
beta_second = 0.99
beta_stats = 0.95
learn_rate = 0.02
aux_rate = 0.15
epsilon = 1e-08
decay_weight = 0.01
early_weight = 0.5


def with_halo(cells, sides, width):
    for axis, dim in sides:
        count = lax.axis_size(axis)
        ends = count - 1
        head = lax.slice_in_dim(cells, 0, width, axis=dim)
        tail = lax.slice_in_dim(cells, cells.shape[dim] - width, cells.shape[dim], axis=dim)
        cells = jnp.concatenate(
            [
                lax.ppermute(tail, axis, [(i, (i + 1) % count) for i in range(ends)]),
                cells,
                lax.ppermute(head, axis, [((i + 1) % count, i) for i in range(ends)]),
            ],
            axis=dim,
        )
    return cells


def full_dot(matrix_a, matrix_b):
    return jnp.dot(matrix_a, matrix_b, precision=highest, preferred_element_type=jnp.float32)


def half_dot(matrix_a, matrix_b):
    return jnp.dot(matrix_a, matrix_b, preferred_element_type=jnp.float32)


def rows_dot(matrix_a, matrix_b, exactness=None):
    return lax.dot_general(
        matrix_a,
        matrix_b,
        (((0,), (0,)), ((), ())),
        precision=exactness,
        preferred_element_type=jnp.float32,
    )


def cols_dot(matrix_a, matrix_b):
    return lax.dot_general(
        matrix_a, matrix_b, (((1,), (1,)), ((), ())), preferred_element_type=jnp.float32
    )


def _nt(x, y, precision=highest):
    return lax.dot_general(x, y, (((1,), (1,)), ((), ())), precision=precision, preferred_element_type=jnp.float32)

def _nn(x, y, precision=highest):
    return lax.dot_general(x, y, (((1,), (0,)), ((), ())), precision=precision, preferred_element_type=jnp.float32)

def _split(x):
    hi = x.astype(jnp.bfloat16)
    return hi, (x - hi.astype(jnp.float32)).astype(jnp.bfloat16)

def _three(dims, x, y):
    xh, xl = x
    yh, yl = y
    dot = lambda a, b: lax.dot_general(a, b, dims, preferred_element_type=jnp.float32)
    return dot(xh, yh) + (dot(xh, yl) + dot(xl, yh))

NT = (((1,), (1,)), ((), ()))
NN = (((1,), (0,)), ((), ()))

def pair_inverse(blocks):
    lane = lax.broadcasted_iota(jnp.int32, (8, 128), 1)
    sub = lax.broadcasted_iota(jnp.int32, (8, 128), 0)
    local = lane % 64
    half = lane - local
    groups = [[block[8 * g:8 * g + 8] for g in range(8)] for block in blocks]
    for start in range(0, 64, 4):
        first, low = divmod(start, 8)
        inside = (local >= start) & (local < start + 4)
        for rows in groups:
            cols = []
            for n in range(4):
                pick = half + (start + n)
                cols.append([jnp.take_along_axis(rows[g], pick, axis=1, mode="promise_in_bounds") for g in range(first, 8)])
            lead = rows[first]
            entry = [[cols[n][0][low + m:low + m + 1] for n in range(m + 1)] for m in range(4)]
            work = [jnp.where(local == start + m, 1.0, jnp.where(inside, 0.0, jnp.broadcast_to(lead[low + m:low + m + 1], (8, 128)))) for m in range(4)]
            entry = [[jnp.broadcast_to(e, (8, 128)) for e in line] for line in entry]
            scaled = []
            ratio = {}
            for m in range(4):
                inverse = 1.0 / entry[m][m]
                for n in range(m + 1, 4):
                    ratio[n, m] = entry[n][m] * inverse
                for n in range(m + 1, 4):
                    work[n] = work[n] - ratio[n, m] * work[m]
                    for q in range(m + 1, n + 1):
                        entry[n][q] = entry[n][q] - ratio[n, m] * entry[q][m]
                scaled.append(work[m] * inverse)
            final = [work[m] * lax.rsqrt(entry[m][m]) for m in range(4)]
            for m in (2, 1, 0):
                for n in range(m + 1, 4):
                    scaled[m] = scaled[m] - ratio[n, m] * scaled[n]
            for g in range(first, 8):
                old = jnp.where(inside, 0.0, rows[g])
                new = old
                for n in range(4):
                    new = new - cols[n][g - first] * scaled[n]
                if g == first:
                    kept = rows[g]
                    for m in range(4):
                        kept = jnp.where(sub == low + m, final[m], kept)
                    new = jnp.where(sub >= low + 4, new, kept)
                rows[g] = new
    return [
        jnp.concatenate([jnp.where(local <= 8 * g + sub, rows[g], 0.0) for g in range(8)], axis=0)
        for rows in groups
    ]

def beside(x, y):
    return jnp.concatenate([x, y], axis=1)

def paired(block):
    wide = jnp.concatenate([block, block], axis=0)
    row = lax.broadcasted_iota(jnp.int32, (128, 128), 0)
    col = lax.broadcasted_iota(jnp.int32, (128, 128), 1)
    return jnp.where((row // 64) == (col // 64), wide, 0.0)

def factor_kernel(gram_ref, tall_ref, out_ref, s_ref, a_ref, y_ref, l_ref, w_ref):
    count = gram_ref.shape[0]
    step = pl.program_id(0)

    @pl.when(step == 0)
    def _():
        s_ref[...] = gram_ref[...]
        a_ref[...] = tall_ref[...]

    start = pl.multiple_of(step * 128, 128)
    diag = [s_ref[i, pl.ds(start, 128), pl.ds(start, 128)] for i in range(count)]
    pairs = range(count // 2)
    top = pair_inverse([beside(diag[2 * p][:64, :64], diag[2 * p + 1][:64, :64]) for p in pairs])
    cross, below = [], []
    for p in pairs:
        low = beside(diag[2 * p][64:, :64], diag[2 * p + 1][64:, :64])
        factor = _nt(low, paired(top[p]))
        cross.append(factor)
        rest = beside(diag[2 * p][64:, 64:], diag[2 * p + 1][64:, 64:])
        below.append(rest - _nt(factor, paired(factor)))
    bottom = pair_inverse(below)
    for p in pairs:
        corner = -_nn(_nn(bottom[p], paired(cross[p])), paired(top[p]))
        zero = jnp.zeros((64, 64), jnp.float32)
        for side in range(2):
            cut = slice(64 * side, 64 * side + 64)
            w_ref[2 * p + side, :64] = beside(top[p][:, cut], zero)
            w_ref[2 * p + side, 64:] = beside(corner[:, cut], bottom[p][:, cut])

    @pl.when(step % 2 == 0)
    def _():
        for i in range(count):
            inv = w_ref[i]
            y_ref[i, :128, :128] = inv
            y_ref[i, :128, 128:] = jnp.zeros((128, 128), jnp.float32)
            low = s_ref[i, pl.ds(start + 128, 128), pl.ds(start, 128)]
            factor = _nt(low, inv)
            l_ref[i] = factor
            s_ref[i, pl.ds(start + 128, 128), pl.ds(start + 128, 128)] -= _nt(factor, factor)

    @pl.when(step % 2 == 1)
    def _():
        for i in range(count):
            inv = w_ref[i]
            y_ref[i, 128:, :128] = -_nn(_nn(inv, l_ref[i]), y_ref[i, :128, :128])
            y_ref[i, 128:, 128:] = inv

    @pl.when(step == 1)
    def _():
        for i in range(count):
            inv = y_ref[i]
            factor = _nt(s_ref[i, 256:, :256], inv)
            s_ref[i, 256:, 256:] -= _nt(factor, factor)
            inv = _split(inv)
            done = _three(NT, _split(a_ref[i, :, :256]), inv)
            out_ref[i, :, :256] = done
            a_ref[i, :, 256:] -= _three(NT, _split(done), _split(factor))

    @pl.when(step == 3)
    def _():
        for i in range(count):
            out_ref[i, :, 256:] = _three(NT, _split(a_ref[i, :, 256:]), _split(y_ref[i]))

def orthonormal_all(gram, tall):
    count = gram.shape[0]
    whole = lambda: pl.BlockSpec(memory_space=pltpu.VMEM)
    return pl.pallas_call(
        factor_kernel,
        grid=(4,),
        out_shape=jax.ShapeDtypeStruct(tall.shape, jnp.float32),
        in_specs=[whole(), whole()],
        out_specs=whole(),
        scratch_shapes=[
            pltpu.VMEM((count, 512, 512), jnp.float32),
            pltpu.VMEM((count, 512, 512), jnp.float32),
            pltpu.VMEM((count, 256, 256), jnp.float32),
            pltpu.VMEM((count, 128, 128), jnp.float32),
            pltpu.VMEM((count, 128, 128), jnp.float32),
        ],
    )(gram, tall)


def high_dot(matrix_a, matrix_b, dims):
    return lax.dot_general(
        matrix_a, matrix_b, dims, precision=lax.Precision.HIGH, preferred_element_type=jnp.float32
    )


def low_dot(matrix_a, matrix_b, dims):
    return lax.dot_general(
        matrix_a.astype(jnp.bfloat16),
        matrix_b.astype(jnp.bfloat16),
        dims,
        preferred_element_type=jnp.float32,
    )


PLAIN = (((2,), (1,)), ((0,), (0,)))
FIRST = (((1,), (1,)), ((0,), (0,)))
SECOND = (((2,), (2,)), ((0,), (0,)))


def soap_update(
    weight,
    gradient,
    moment_one,
    moment_two,
    left_stats,
    right_stats,
    left_basis,
    right_basis,
    steps_done,
):
    owned = weight.shape[0]
    turned = high_dot(left_basis, gradient.astype(jnp.float32), FIRST)
    rotated = high_dot(turned, right_basis, PLAIN)
    moment_one = beta_first * moment_one + (1.0 - beta_first) * rotated
    moment_two = beta_second * moment_two + (1.0 - beta_second) * rotated * rotated
    direction = (
        moment_one
        / (1.0 - beta_first**steps_done)
        / (jnp.sqrt(moment_two / (1.0 - beta_second**steps_done)) + epsilon)
    )
    weight = weight - learn_rate * (
        low_dot(low_dot(left_basis, direction, PLAIN), right_basis, SECOND) + decay_weight * weight
    )
    left_stats = beta_stats * left_stats + (1.0 - beta_stats) * low_dot(gradient, gradient, SECOND)
    right_stats = beta_stats * right_stats + (1.0 - beta_stats) * low_dot(gradient, gradient, FIRST)
    tall = jnp.concatenate(
        [high_dot(left_stats, left_basis, PLAIN), high_dot(right_stats, right_basis, PLAIN)], axis=0
    )
    bases = orthonormal_all(high_dot(tall, tall, FIRST), tall)
    left_new, right_new = bases[:owned], bases[owned:]
    initial = high_dot(high_dot(left_basis, moment_one, PLAIN), right_basis, SECOND)
    moment_one = high_dot(high_dot(left_new, initial, FIRST), right_new, PLAIN)
    return (weight, moment_one, moment_two, left_stats, right_stats, left_new, right_new)


def swap(values, axis, bit):
    return lax.ppermute(values, axis, [(i, i ^ bit) for i in range(lax.axis_size(axis))])


def side_of(axis, bit):
    return (lax.axis_index(axis) // bit) % 2


def ordered(values, others, axis, bit, dim):
    first = side_of(axis, bit) == 0
    return jnp.concatenate(
        [jnp.where(first, values, others), jnp.where(first, others, values)], axis=dim
    )


def halves(values, axis, bit, dim):
    width = values.shape[dim] // 2
    side = side_of(axis, bit)
    return (
        lax.dynamic_slice_in_dim(values, side * width, width, dim),
        lax.dynamic_slice_in_dim(values, (1 - side) * width, width, dim),
    )


def bits_of(axis):
    count = lax.axis_size(axis)
    return [1 << i for i in range(count.bit_length() - 1)]


def scatter_half(values, axis, bit, dim):
    kept, sent = halves(values, axis, bit, dim)
    return kept + swap(sent, axis, bit)


def all_sum(values):
    for axis in ("opt", "tm"):
        for bit in bits_of(axis):
            values = values + swap(values, axis, bit)
    return values


def gather_blocks(values, axis, bits):
    for bit in bits:
        values = ordered(values, swap(values, axis, bit), axis, bit, 0)
    return values


def reduce_slots(own_core, owned):
    pieces = []
    low = own_core.astype(jnp.bfloat16)
    kept, sent = halves(low, "opt", 1, 1)
    low = (kept + swap(sent, "opt", 1))[:, 0]
    kept, sent = halves(low, "opt", 2, 0)
    for slot in range(owned):
        part = kept[0, slot] + swap(sent[0, slot], "opt", 2)
        bits = bits_of("tm")
        for bit in bits[:-1]:
            part = scatter_half(part, "tm", bit, 0)
        part = part + swap(part, "tm", bits[-1])
        for bit in reversed(bits[:-1]):
            part = ordered(part, swap(part, "tm", bit), "tm", bit, 0)
        pieces.append(part)
    return jnp.stack(pieces)


def adamw_update(weight, gradient, moment_one, moment_two, steps_done, rate_value):
    moment_one = beta_first * moment_one + (1.0 - beta_first) * gradient
    moment_two = beta_second * moment_two + (1.0 - beta_second) * gradient * gradient
    direction = (
        moment_one
        / (1.0 - beta_first**steps_done)
        / (jnp.sqrt(moment_two / (1.0 - beta_second**steps_done)) + epsilon)
    )
    weight = weight - rate_value * (direction + decay_weight * weight)
    return (weight, moment_one, moment_two)


def gate_parts(before_gate):
    half_width = before_gate.shape[1] // 2
    return (jnp.tanh(before_gate[:, :half_width]), jax.nn.sigmoid(before_gate[:, half_width:]))


def layer_forward(
    hidden_state, conditioning_part, bias_vector_row, taps, dilation_step, crops_current
):
    row_count, channels = hidden_state.shape
    length = row_count // crops_current
    hidden_low = hidden_state.astype(jnp.bfloat16).reshape(crops_current, length, channels)
    padded_input = with_halo(hidden_low, (("tm", 1),), dilation_step)
    before_gate = conditioning_part + bias_vector_row
    for k in range(3):
        window = padded_input[:, k * dilation_step : k * dilation_step + length].reshape(
            row_count, channels
        )
        before_gate = before_gate + half_dot(window, taps[k])
    tangent, sigmoid_part = gate_parts(before_gate)
    gated = (tangent * sigmoid_part).astype(jnp.bfloat16)
    return (padded_input, before_gate, gated)


def layer_backward(padded_input, before_gate, taps, gated_gradient, dilation_step):
    crops_current, width_all, channels = padded_input.shape
    length = width_all - 2 * dilation_step
    row_count = crops_current * length
    tangent, sigmoid_part = gate_parts(before_gate)
    grad_before = jnp.concatenate(
        [
            gated_gradient * (1.0 - tangent * tangent) * sigmoid_part,
            gated_gradient * tangent * sigmoid_part * (1.0 - sigmoid_part),
        ],
        axis=1,
    ).astype(jnp.bfloat16)
    tap_grads = []
    grad_padded = jnp.zeros((crops_current, width_all, channels), jnp.float32)
    for k in range(3):
        window = padded_input[:, k * dilation_step : k * dilation_step + length].reshape(
            row_count, channels
        )
        tap_grads.append(rows_dot(window, grad_before))
        flowing = cols_dot(grad_before, taps[k]).reshape(crops_current, length, channels)
        grad_padded = grad_padded.at[:, k * dilation_step : k * dilation_step + length].add(flowing)
    rims = jnp.concatenate(
        [grad_padded[:, :dilation_step], grad_padded[:, length + dilation_step :]], axis=1
    )
    extended = with_halo(rims, (("tm", 1),), dilation_step)
    core = grad_padded[:, dilation_step : dilation_step + length]
    core = core.at[:, :dilation_step].add(extended[:, :dilation_step])
    core = core.at[:, length - dilation_step :].add(extended[:, 3 * dilation_step :])
    return (grad_before, jnp.stack(tap_grads), core.reshape(row_count, channels))


def shards(
    wave,
    crop_offsets,
    squeeze_order,
    mel,
    mel_index,
    soap_slots,
    step_count,
    in_weight,
    soap_first,
    soap_second,
    left_stats,
    right_stats,
    left_basis,
    right_basis,
    cond_weight,
    cond_first,
    cond_second,
    out_weight,
    out_first,
    out_second,
    aux_params,
    aux_first,
    aux_second,
    flow_params,
    flow_first,
    flow_second,
):
    crops_current = wave.shape[0]
    row_count = crops_current * G_DEV
    tokens_all = row_count * lax.axis_size("tm") * lax.axis_size("opt")
    scale_final = 1.0 / (6.0 * tokens_all)
    scale_early = early_weight / (2.0 * tokens_all)
    steps_done = step_count[0].astype(jnp.float32)
    owned = NMAT // lax.axis_size("opt")
    opt_bits, tm_bits = bits_of("opt"), bits_of("tm")
    own = in_weight.astype(jnp.bfloat16)
    across = swap(own, "opt", 2)
    own_x = ordered(own[None], swap(own, "opt", 1)[None], "opt", 1, 0)
    other_x = ordered(across[None], swap(across, "opt", 1)[None], "opt", 1, 0)
    slot_weights = ordered(own_x, other_x, "opt", 2, 0).reshape(NMAT, H, H)
    matrices = jnp.take(slot_weights, jnp.argsort(soap_slots), axis=0)
    every_tap_weight = jnp.transpose(matrices.reshape(LAYERS, 3, 2, H, H), (0, 1, 3, 2, 4)).reshape(
        LAYERS, 3, H, 2 * H
    )
    cond_part = cond_weight.astype(jnp.bfloat16)
    cond_part = ordered(cond_part, swap(cond_part, "opt", 2), "opt", 2, 1)
    cond_part = gather_blocks(cond_part, "tm", tm_bits)
    cond_other = swap(cond_part, "opt", 1)
    cond_rows = cond_part.shape[0]
    cond_full = ordered(
        cond_part.reshape(cond_rows, 2, 1, -1), cond_other.reshape(cond_rows, 2, 1, -1), "opt", 1, 2
    ).reshape(cond_rows, -1)
    out_part = jnp.swapaxes(out_weight.astype(jnp.bfloat16), 0, 1)
    out_part = ordered(out_part, swap(out_part, "opt", 2), "opt", 2, 2)
    out_part = gather_blocks(out_part, "tm", tm_bits)
    out_other = swap(out_part, "opt", 1)
    out_full = ordered(
        out_part.reshape(H, 3, 2, 1, -1), out_other.reshape(H, 3, 2, 1, -1), "opt", 1, 3
    ).reshape(H, 3, H)
    out_full = jnp.swapaxes(out_full, 0, 1)

    def squeeze_one(samples, offset):
        segment = lax.dynamic_slice_in_dim(samples, offset, 8 * G_DEV, 0)
        return jnp.take(segment.reshape(G_DEV, 8), squeeze_order, axis=1)

    squeezed = jax.vmap(squeeze_one)(wave[:, 0], crop_offsets).reshape(row_count, 8)
    frames_hit = (mel_index[..., None] == jnp.arange(FR_DEV, dtype=jnp.int32)).astype(jnp.bfloat16)
    conditioning = (
        jnp.einsum("cgjf,cfm->cgjm", frames_hit, mel, preferred_element_type=jnp.float32)
        .astype(jnp.bfloat16)
        .reshape(row_count, 8 * MEL)
    )
    spectral = cols_dot(conditioning, cond_full)
    flow_matrix = flow_params[:, :6]
    mixed = full_dot(squeezed[:, 2:], flow_matrix.T)
    lower_half = mixed[:, :3]
    upper_half = mixed[:, 3:]
    hidden_state = full_dot(lower_half, aux_params[0:3]) + aux_params[3]
    skip_total = jnp.zeros((row_count, H), jnp.float32)
    bias_base = 4 + 2 * LAYERS
    saved = []
    for layer_number in range(LAYERS):
        bias_vector_row = aux_params[4 + 2 * layer_number : 6 + 2 * layer_number].reshape(2 * H)
        conditioning_part = spectral[:, 2 * H * layer_number : 2 * H * (layer_number + 1)]
        padded_input, before_gate, gated = layer_forward(
            hidden_state,
            conditioning_part,
            bias_vector_row,
            every_tap_weight[layer_number],
            FIRST_DILATION * 2**layer_number,
            crops_current,
        )
        if layer_number < LAYERS - 1:
            hidden_state = (
                hidden_state
                + half_dot(gated, out_full[layer_number])
                + aux_params[bias_base + layer_number]
            )
        skip_total = (
            skip_total
            + half_dot(gated, out_full[LAYERS - 1 + layer_number])
            + aux_params[bias_base + LAYERS - 1 + layer_number]
        )
        saved.append((padded_input, before_gate, gated))
    end_weight = aux_params[4 * LAYERS + 3 :]
    outputs = full_dot(skip_total, end_weight.T) + flow_params[:, 6]
    log_scale = outputs[:, :3]
    growth = jnp.exp(log_scale)
    z_upper = growth * upper_half + outputs[:, 3:]
    final_part = (
        0.5 * jnp.sum(lower_half * lower_half)
        + 0.5 * jnp.sum(z_upper * z_upper)
        - jnp.sum(log_scale)
    )
    early_part = 0.5 * jnp.sum(squeezed[:, :2] * squeezed[:, :2])
    grad_upper_z = scale_final * z_upper
    grad_outputs = jnp.concatenate(
        [grad_upper_z * growth * upper_half - scale_final, grad_upper_z], axis=1
    )
    grad_upper = grad_upper_z * growth
    grad_end = rows_dot(grad_outputs, skip_total, highest)
    grad_end_bias = jnp.sum(grad_outputs, axis=0)
    grad_skip = full_dot(grad_outputs, end_weight).astype(jnp.bfloat16)
    grad_hidden = jnp.zeros((row_count, H), jnp.float32)
    out_grads = [None] * (2 * LAYERS - 1)
    out_bias_grads = [None] * (2 * LAYERS - 1)
    in_bias_grads = [None] * LAYERS
    tap_grads = [None] * LAYERS
    spectral_grads = [None] * LAYERS
    for layer_number in reversed(range(LAYERS)):
        padded_input, before_gate, gated = saved[layer_number]
        skip_index = LAYERS - 1 + layer_number
        gated_gradient = cols_dot(grad_skip, out_full[skip_index])
        out_grads[skip_index] = rows_dot(gated, grad_skip)
        out_bias_grads[skip_index] = jnp.sum(grad_skip.astype(jnp.float32), axis=0)
        if layer_number < LAYERS - 1:
            grad_residual = grad_hidden.astype(jnp.bfloat16)
            gated_gradient = gated_gradient + cols_dot(grad_residual, out_full[layer_number])
            out_grads[layer_number] = rows_dot(gated, grad_residual)
            out_bias_grads[layer_number] = jnp.sum(grad_residual.astype(jnp.float32), axis=0)
        grad_before, tap_grads[layer_number], grad_conv = layer_backward(
            padded_input,
            before_gate,
            every_tap_weight[layer_number],
            gated_gradient,
            FIRST_DILATION * 2**layer_number,
        )
        in_bias_grads[layer_number] = jnp.sum(grad_before.astype(jnp.float32), axis=0)
        spectral_grads[layer_number] = grad_before
        grad_hidden = grad_hidden + grad_conv
    grad_start = rows_dot(lower_half, grad_hidden, highest)
    grad_start_bias = jnp.sum(grad_hidden, axis=0)
    grad_lower = scale_final * lower_half + full_dot(grad_hidden, aux_params[0:3].T)
    grad_mixed = jnp.concatenate([grad_lower, grad_upper], axis=1)
    grad_flow = jnp.concatenate(
        [rows_dot(grad_mixed, squeezed[:, 2:], highest), grad_end_bias[:, None]], axis=1
    )
    grad_aux = jnp.concatenate(
        [
            grad_start,
            grad_start_bias[None],
            jnp.stack(in_bias_grads).reshape(2 * LAYERS, H),
            jnp.stack(out_bias_grads),
            grad_end,
        ],
        axis=0,
    )
    small = jnp.concatenate(
        [grad_aux.reshape(-1), grad_flow.reshape(-1), jnp.stack([final_part, early_part])]
    )
    filled = small.shape[0]
    small = jnp.pad(small, (0, -filled % 1024)).reshape(-1, 128)
    small = all_sum(small).reshape(-1)
    grad_aux = small[: grad_aux.size].reshape(grad_aux.shape)
    grad_flow = small[grad_aux.size : filled - 2].reshape(grad_flow.shape)
    parts = small[filled - 2 : filled]
    factor = jnp.linalg.cholesky(full_dot(flow_matrix, flow_matrix.T))
    log_det = jnp.sum(jnp.log(jnp.diagonal(factor)))
    inverse_t = jax.scipy.linalg.cho_solve((factor, True), flow_matrix)
    grad_flow = grad_flow.at[:, :6].add(-inverse_t / 6.0)
    loss = parts[0] * scale_final + parts[1] * scale_early - log_det / 6.0
    grad_cond = rows_dot(jnp.concatenate(spectral_grads, axis=1), conditioning)
    grad_cond = grad_cond.astype(jnp.bfloat16).reshape(4 * H, 2, 2, -1)
    grad_out = jnp.stack(out_grads).astype(jnp.bfloat16).reshape(3, H, 2, 2, -1)
    grad_cond = scatter_half(grad_cond, "opt", 1, 2)
    grad_out = scatter_half(grad_out, "opt", 1, 3)
    grad_cond = scatter_half(grad_cond, "opt", 2, 1)
    grad_out = scatter_half(grad_out, "opt", 2, 2)
    grad_cond = grad_cond.reshape(4 * H, -1)
    grad_out = grad_out.reshape(3, H, -1)
    for bit in reversed(tm_bits):
        grad_cond = scatter_half(grad_cond, "tm", bit, 0)
        grad_out = scatter_half(grad_out, "tm", bit, 1)
    grad_cond, grad_out = grad_cond.astype(jnp.float32), grad_out.astype(jnp.float32)
    grad_taps = jnp.stack(tap_grads).reshape(LAYERS, 3, H, 2, H)
    grad_matrices = jnp.transpose(grad_taps, (0, 1, 3, 2, 4)).reshape(NMAT, H, H)
    grad_slots = jnp.take(grad_matrices, soap_slots, axis=0)
    grad_owned = reduce_slots(grad_slots.reshape(2, 2, owned, H, H), owned)
    (
        in_new,
        soap_first_new,
        soap_second_new,
        left_stats_new,
        right_stats_new,
        left_basis_new,
        right_basis_new,
    ) = soap_update(
        in_weight,
        grad_owned,
        soap_first,
        soap_second,
        left_stats,
        right_stats,
        left_basis,
        right_basis,
        steps_done,
    )
    cond_new, cond_first_new, cond_second_new = adamw_update(
        cond_weight, grad_cond, cond_first, cond_second, steps_done, learn_rate
    )
    out_new, out_first_new, out_second_new = adamw_update(
        out_weight, grad_out, out_first, out_second, steps_done, learn_rate
    )
    aux_new, aux_first_new, aux_second_new = adamw_update(
        aux_params, grad_aux, aux_first, aux_second, steps_done, aux_rate
    )
    flow_new, flow_first_new, flow_second_new = adamw_update(
        flow_params, grad_flow, flow_first, flow_second, steps_done, learn_rate
    )
    return (
        loss,
        in_new,
        soap_first_new,
        soap_second_new,
        left_stats_new,
        right_stats_new,
        left_basis_new,
        right_basis_new,
        cond_new,
        cond_first_new,
        cond_second_new,
        out_new,
        out_first_new,
        out_second_new,
        aux_new,
        aux_first_new,
        aux_second_new,
        flow_new,
        flow_first_new,
        flow_second_new,
    )


def solution(mesh):
    placed = (
        P("opt", "tm", None),
        P("opt"),
        P(),
        P("opt", "tm", None),
        P("opt", "tm", None),
        P(),
        P(),
        P("opt", None, None),
        P("opt", None, None),
        P("opt", None, None),
        P("opt", None, None),
        P("opt", None, None),
        P("opt", None, None),
        P("opt", None, None),
        P("tm", "opt"),
        P("tm", "opt"),
        P("tm", "opt"),
        P(None, "tm", "opt"),
        P(None, "tm", "opt"),
        P(None, "tm", "opt"),
        P(),
        P(),
        P(),
        P(),
        P(),
        P(),
    )
    return jax.shard_map(
        shards,
        mesh=mesh,
        in_specs=placed,
        out_specs=(
            P(),
            P("opt", None, None),
            P("opt", None, None),
            P("opt", None, None),
            P("opt", None, None),
            P("opt", None, None),
            P("opt", None, None),
            P("opt", None, None),
            P("tm", "opt"),
            P("tm", "opt"),
            P("tm", "opt"),
            P(None, "tm", "opt"),
            P(None, "tm", "opt"),
            P(None, "tm", "opt"),
            P(),
            P(),
            P(),
            P(),
            P(),
            P(),
        ),
        check_vma=False,
    )
```

```python
import jax
import jax.numpy as jnp
from jax import lax
from jax.experimental import pallas as pl
from jax.experimental.pallas import tpu as pltpu
from jax.sharding import PartitionSpec as P

H = 512
MEL = 80
LAYERS = 2
FIRST_DILATION = 64
G_DEV = 512
FR_DEV = 16
NMAT = 12


highest = lax.Precision.HIGHEST
beta_first = 0.9
beta_second = 0.99
beta_stats = 0.95
learn_rate = 0.02
aux_rate = 0.15
epsilon = 1e-08
decay_weight = 0.01
early_weight = 0.5


def full_dot(matrix_a, matrix_b):
    return jnp.dot(matrix_a, matrix_b, precision=highest, preferred_element_type=jnp.float32)


def half_dot(matrix_a, matrix_b):
    return jnp.dot(matrix_a, matrix_b, preferred_element_type=jnp.float32)


def rows_dot(matrix_a, matrix_b, exactness=None):
    return lax.dot_general(
        matrix_a,
        matrix_b,
        (((0,), (0,)), ((), ())),
        precision=exactness,
        preferred_element_type=jnp.float32,
    )


def cols_dot(matrix_a, matrix_b):
    return lax.dot_general(
        matrix_a, matrix_b, (((1,), (1,)), ((), ())), preferred_element_type=jnp.float32
    )


def _nt(x, y, precision=highest):
    return lax.dot_general(x, y, (((1,), (1,)), ((), ())), precision=precision, preferred_element_type=jnp.float32)

def _nn(x, y, precision=highest):
    return lax.dot_general(x, y, (((1,), (0,)), ((), ())), precision=precision, preferred_element_type=jnp.float32)

def _split(x):
    hi = x.astype(jnp.bfloat16)
    return hi, (x - hi.astype(jnp.float32)).astype(jnp.bfloat16)

def _three(dims, x, y):
    xh, xl = x
    yh, yl = y
    dot = lambda a, b: lax.dot_general(a, b, dims, preferred_element_type=jnp.float32)
    return dot(xh, yh) + (dot(xh, yl) + dot(xl, yh))

NT = (((1,), (1,)), ((), ()))
NN = (((1,), (0,)), ((), ()))

def pair_inverse(blocks):
    lane = lax.broadcasted_iota(jnp.int32, (8, 128), 1)
    sub = lax.broadcasted_iota(jnp.int32, (8, 128), 0)
    local = lane % 64
    half = lane - local
    groups = [[block[8 * g:8 * g + 8] for g in range(8)] for block in blocks]
    for start in range(0, 64, 4):
        first, low = divmod(start, 8)
        inside = (local >= start) & (local < start + 4)
        for rows in groups:
            cols = []
            for n in range(4):
                pick = half + (start + n)
                cols.append([jnp.take_along_axis(rows[g], pick, axis=1, mode="promise_in_bounds") for g in range(first, 8)])
            lead = rows[first]
            entry = [[cols[n][0][low + m:low + m + 1] for n in range(m + 1)] for m in range(4)]
            work = [jnp.where(local == start + m, 1.0, jnp.where(inside, 0.0, jnp.broadcast_to(lead[low + m:low + m + 1], (8, 128)))) for m in range(4)]
            entry = [[jnp.broadcast_to(e, (8, 128)) for e in line] for line in entry]
            scaled = []
            ratio = {}
            for m in range(4):
                inverse = 1.0 / entry[m][m]
                for n in range(m + 1, 4):
                    ratio[n, m] = entry[n][m] * inverse
                for n in range(m + 1, 4):
                    work[n] = work[n] - ratio[n, m] * work[m]
                    for q in range(m + 1, n + 1):
                        entry[n][q] = entry[n][q] - ratio[n, m] * entry[q][m]
                scaled.append(work[m] * inverse)
            final = [work[m] * lax.rsqrt(entry[m][m]) for m in range(4)]
            for m in (2, 1, 0):
                for n in range(m + 1, 4):
                    scaled[m] = scaled[m] - ratio[n, m] * scaled[n]
            for g in range(first, 8):
                old = jnp.where(inside, 0.0, rows[g])
                new = old
                for n in range(4):
                    new = new - cols[n][g - first] * scaled[n]
                if g == first:
                    kept = rows[g]
                    for m in range(4):
                        kept = jnp.where(sub == low + m, final[m], kept)
                    new = jnp.where(sub >= low + 4, new, kept)
                rows[g] = new
    return [
        jnp.concatenate([jnp.where(local <= 8 * g + sub, rows[g], 0.0) for g in range(8)], axis=0)
        for rows in groups
    ]

def beside(x, y):
    return jnp.concatenate([x, y], axis=1)

def paired(block):
    wide = jnp.concatenate([block, block], axis=0)
    row = lax.broadcasted_iota(jnp.int32, (128, 128), 0)
    col = lax.broadcasted_iota(jnp.int32, (128, 128), 1)
    return jnp.where((row // 64) == (col // 64), wide, 0.0)

def factor_kernel(
    gram_left, gram_right, tall_left, tall_right, out_left, out_right, s_ref, a_ref, y_ref, l_ref, w_ref
):
    owned = gram_left.shape[0]
    count = 2 * owned
    outs = [out_left.at[i] for i in range(owned)] + [out_right.at[i] for i in range(owned)]
    step = pl.program_id(0)

    @pl.when(step == 0)
    def _():
        s_ref[:owned] = gram_left[...]
        s_ref[owned:] = gram_right[...]
        a_ref[:owned] = tall_left[...]
        a_ref[owned:] = tall_right[...]

    start = pl.multiple_of(step * 128, 128)
    diag = [s_ref[i, pl.ds(start, 128), pl.ds(start, 128)] for i in range(count)]
    pairs = range(count // 2)
    top = pair_inverse([beside(diag[2 * p][:64, :64], diag[2 * p + 1][:64, :64]) for p in pairs])
    cross, below = [], []
    for p in pairs:
        low = beside(diag[2 * p][64:, :64], diag[2 * p + 1][64:, :64])
        factor = _nt(low, paired(top[p]))
        cross.append(factor)
        rest = beside(diag[2 * p][64:, 64:], diag[2 * p + 1][64:, 64:])
        below.append(rest - _nt(factor, paired(factor)))
    bottom = pair_inverse(below)
    for p in pairs:
        corner = -_nn(_nn(bottom[p], paired(cross[p])), paired(top[p]))
        zero = jnp.zeros((64, 64), jnp.float32)
        for side in range(2):
            cut = slice(64 * side, 64 * side + 64)
            w_ref[2 * p + side, :64] = beside(top[p][:, cut], zero)
            w_ref[2 * p + side, 64:] = beside(corner[:, cut], bottom[p][:, cut])

    @pl.when(step % 2 == 0)
    def _():
        for i in range(count):
            inv = w_ref[i]
            y_ref[i, :128, :128] = inv
            y_ref[i, :128, 128:] = jnp.zeros((128, 128), jnp.float32)
            low = s_ref[i, pl.ds(start + 128, 128), pl.ds(start, 128)]
            factor = _nt(low, inv)
            l_ref[i] = factor
            s_ref[i, pl.ds(start + 128, 128), pl.ds(start + 128, 128)] -= _nt(factor, factor)

    @pl.when(step % 2 == 1)
    def _():
        for i in range(count):
            inv = w_ref[i]
            y_ref[i, 128:, :128] = -_nn(_nn(inv, l_ref[i]), y_ref[i, :128, :128])
            y_ref[i, 128:, 128:] = inv

    @pl.when(step == 1)
    def _():
        for i in range(count):
            inv = y_ref[i]
            factor = _nt(s_ref[i, 256:, :256], inv)
            s_ref[i, 256:, 256:] -= _nt(factor, factor)
            inv = _split(inv)
            done = _three(NT, _split(a_ref[i, :, :256]), inv)
            outs[i][:, :256] = done
            a_ref[i, :, 256:] -= _three(NT, _split(done), _split(factor))

    @pl.when(step == 3)
    def _():
        for i in range(count):
            outs[i][:, 256:] = _three(NT, _split(a_ref[i, :, 256:]), _split(y_ref[i]))

def orthonormal_all(grams, talls):
    count = 2 * grams[0].shape[0]
    whole = lambda: pl.BlockSpec(memory_space=pltpu.VMEM)
    return pl.pallas_call(
        factor_kernel,
        grid=(4,),
        out_shape=[jax.ShapeDtypeStruct(tall.shape, jnp.float32) for tall in talls],
        in_specs=[whole() for _ in range(4)],
        out_specs=[whole(), whole()],
        scratch_shapes=[
            pltpu.VMEM((count, 512, 512), jnp.float32),
            pltpu.VMEM((count, 512, 512), jnp.float32),
            pltpu.VMEM((count, 256, 256), jnp.float32),
            pltpu.VMEM((count, 128, 128), jnp.float32),
            pltpu.VMEM((count, 128, 128), jnp.float32),
        ],
        name="orthonormal",
    )(*grams, *talls)


def high_dot(matrix_a, matrix_b, dims):
    return lax.dot_general(
        matrix_a, matrix_b, dims, precision=lax.Precision.HIGH, preferred_element_type=jnp.float32
    )


def low_dot(matrix_a, matrix_b, dims):
    return lax.dot_general(
        matrix_a.astype(jnp.bfloat16),
        matrix_b.astype(jnp.bfloat16),
        dims,
        preferred_element_type=jnp.float32,
    )


PLAIN = (((2,), (1,)), ((0,), (0,)))
FIRST = (((1,), (1,)), ((0,), (0,)))
SECOND = (((2,), (2,)), ((0,), (0,)))


def soap_update(
    weight,
    gradient,
    moment_one,
    moment_two,
    left_stats,
    right_stats,
    left_basis,
    right_basis,
    steps_done,
    along,
):
    owned = weight.shape[0]
    turned = high_dot(left_basis, gradient.astype(jnp.float32), FIRST)
    rotated = high_dot(turned, right_basis, PLAIN)
    moment_one = beta_first * moment_one + (1.0 - beta_first) * rotated
    moment_two = beta_second * moment_two + (1.0 - beta_second) * rotated * rotated
    direction = (
        moment_one
        / (1.0 - beta_first**steps_done)
        / (jnp.sqrt(moment_two / (1.0 - beta_second**steps_done)) + epsilon)
    )
    weight = weight - learn_rate * (
        low_dot(low_dot(left_basis, direction, PLAIN), right_basis, SECOND) + decay_weight * weight
    )
    left_stats = beta_stats * left_stats + (1.0 - beta_stats) * low_dot(gradient, gradient, SECOND)
    right_stats = beta_stats * right_stats + (1.0 - beta_stats) * low_dot(gradient, gradient, FIRST)
    talls = (high_dot(left_stats, left_basis, PLAIN), high_dot(right_stats, right_basis, PLAIN))
    grams = tuple(high_dot(tall, tall, FIRST) for tall in talls)
    grams, along = lax.optimization_barrier((grams, along))
    left_new, right_new = orthonormal_all(grams, talls)
    initial = high_dot(high_dot(left_basis, moment_one, PLAIN), right_basis, SECOND)
    moment_one = high_dot(high_dot(left_new, initial, FIRST), right_new, PLAIN)
    return (weight, moment_one, moment_two, left_stats, right_stats, left_new, right_new, along)


def swap(values, axis, bit):
    return lax.ppermute(values, axis, [(i, i ^ bit) for i in range(lax.axis_size(axis))])


def side_of(axis, bit):
    return (lax.axis_index(axis) // bit) % 2


def ordered(values, others, axis, bit, dim):
    first = side_of(axis, bit) == 0
    return jnp.concatenate(
        [jnp.where(first, values, others), jnp.where(first, others, values)], axis=dim
    )


def halves(values, axis, bit, dim):
    width = values.shape[dim] // 2
    side = side_of(axis, bit)
    return (
        lax.dynamic_slice_in_dim(values, side * width, width, dim),
        lax.dynamic_slice_in_dim(values, (1 - side) * width, width, dim),
    )


def bits_of(axis):
    count = lax.axis_size(axis)
    return [1 << i for i in range(count.bit_length() - 1)]


def scatter_half(values, axis, bit, dim):
    kept, sent = halves(values, axis, bit, dim)
    return kept + swap(sent, axis, bit)


def all_sum(values):
    for axis in ("opt", "tm"):
        for bit in bits_of(axis):
            values = values + swap(values, axis, bit)
    return values


def gather_blocks(values, axis, bits):
    for bit in bits:
        values = ordered(values, swap(values, axis, bit), axis, bit, 0)
    return values


ROWS = 256
DNT = (((1,), (1,)), ((), ()))
DTN = (((0,), (0,)), ((), ()))


def dot_as(dims, x, y):
    return lax.dot_general(x, y, dims, preferred_element_type=jnp.float32)


def fetch_taps(place_ref, sources, taps_ref, sem, layer):
    owned = sources[0].shape[0]
    for j in range(6):
        place = place_ref[6 * layer + j]
        for r, source in enumerate(sources):

            @pl.when(place // owned == r)
            def _(source=source):
                pltpu.make_async_copy(source.at[place % owned], taps_ref.at[j], sem.at[j]).start()


def await_taps(sources, taps_ref, sem):
    for j in range(6):
        pltpu.make_async_copy(sources[0].at[0], taps_ref.at[j], sem.at[j]).wait()


def sigmoid(x):
    return 0.5 * jnp.tanh(0.5 * x) + 0.5


def gate_inputs(
    layer, info_ref, cond_refs, weight_refs, aux_ref, crop_ref, crop, base, dilation, taps_ref
):
    sums = []
    for half in range(2):
        parts = []
        for block in range(2):
            spot = info_ref[NMAT + 4 * layer + 2 * half + block]
            part = dot_as(NN, cond_refs[0][...], weight_refs[0][spot])
            parts.append(part + dot_as(NN, cond_refs[1][...], weight_refs[1][spot]))
        total = jnp.concatenate(parts, axis=1) + aux_ref[4 + 2 * layer + half : 5 + 2 * layer + half, :]
        for k in range(3):
            window = crop_ref[crop, pl.ds(base + dilation * k, ROWS), :]
            total = total + dot_as(NN, window, taps_ref[2 * k + half])
        sums.append(total)
    return sums


def start_rows(mixed, aux_ref):
    total = mixed[:, 3:4] * aux_ref[3:4, :]
    for j in range(3):
        total = total + mixed[:, j : j + 1] * aux_ref[j : j + 1, :]
    return total


def first_kernel(
    place_ref, mixed_ref, aux_ref, cond_own, cond_other, rows_own, rows_other, out_own, out_other, w0, w1, w2, w3,
    before_ref, gated_ref, next_ref, start_ref, out_ref, taps_ref, sem,
):
    step = pl.program_id(0)
    sources = (w0, w1, w2, w3)
    per_crop = pl.num_programs(0) // mixed_ref.shape[0]
    margin = FIRST_DILATION

    @pl.when(step == 0)
    def _():
        fetch_taps(place_ref, sources, taps_ref, sem, 0)
        for crop in range(mixed_ref.shape[0]):
            start_ref[crop] = start_rows(mixed_ref[crop], aux_ref).astype(jnp.bfloat16)
        for core, piece in enumerate((out_own, out_other)):
            for across in range(2):
                column = pl.multiple_of(place_ref[NMAT + 8 + 2 * core + across] * 128, 128)
                for t in range(8):
                    spot = place_ref[NMAT + t]
                    for matrix in range(3):
                        out_ref[matrix, 64 * t : 64 * t + 64, pl.ds(column, 128)] = piece[
                            spot, across, matrix
                        ]
        await_taps(sources, taps_ref, sem)

    crop = step // per_crop
    base = pl.multiple_of((step % per_crop) * ROWS, ROWS)
    left, right = gate_inputs(
        0, place_ref, (cond_own, cond_other), (rows_own, rows_other), aux_ref, start_ref, crop, base, margin, taps_ref
    )
    before_ref[:, :H] = left
    before_ref[:, H:] = right
    gated = (jnp.tanh(left) * sigmoid(right)).astype(jnp.bfloat16)
    gated_ref[...] = gated
    hidden = start_rows(mixed_ref[crop, pl.ds(base + margin, ROWS), :], aux_ref)
    hidden = hidden + dot_as(NN, gated, out_ref[0]) + aux_ref[8:9, :]
    next_ref[...] = hidden.astype(jnp.bfloat16)


def second_kernel(
    place_ref, scale_ref, flow_ref, own_ref, before_halo, after_halo, aux_ref, cells_ref,
    cond_own, cond_other, rows_own, rows_other, gated_ref, out_ref, w0, w1, w2, w3,
    skip_ref, grads_ref, low_ref, mixed_ref, sums_ref, taps_ref, wide_ref, end_ref, sem,
):
    step = pl.program_id(0)
    sources = (w0, w1, w2, w3)
    crops, length = own_ref.shape[:2]
    margin = 2 * FIRST_DILATION

    @pl.when(step == 0)
    def _():
        fetch_taps(place_ref, sources, taps_ref, sem, 1)
        wide_ref[:, :margin] = before_halo[...]
        wide_ref[:, margin : margin + length] = own_ref[...]
        wide_ref[:, margin + length :] = after_halo[...]
        sums_ref[...] = jnp.zeros_like(sums_ref)
        end_ref[...] = jnp.zeros_like(end_ref)
        end_ref[0:6] = aux_ref[11:17, :]
        await_taps(sources, taps_ref, sem)

    per_crop = length // ROWS
    crop = step // per_crop
    base = pl.multiple_of((step % per_crop) * ROWS, ROWS)
    left, right = gate_inputs(
        1, place_ref, (cond_own, cond_other), (rows_own, rows_other), aux_ref, wide_ref, crop, base, margin, taps_ref
    )
    tangent, part = jnp.tanh(left), sigmoid(right)
    gated = (tangent * part).astype(jnp.bfloat16)
    skip_ref[...] = gated
    total = dot_as(NN, gated_ref[...], out_ref[1]) + dot_as(NN, gated, out_ref[2])
    total = total + (aux_ref[9:10, :] + aux_ref[10:11, :])
    halves_total = _split(total)
    outputs = _three(DNT, halves_total, _split(end_ref[...]))
    lane = lax.broadcasted_iota(jnp.int32, outputs.shape, 1)
    row_lane = lane[0:1]
    bias = jnp.zeros((1, 128), jnp.float32)
    for j in range(6):
        bias = jnp.where(row_lane == j, flow_ref[j, 6], bias)
    outputs = outputs + bias
    inside = lane < 3
    log_scale = jnp.where(inside, outputs, 0.0)
    growth = jnp.exp(log_scale)
    cells = cells_ref[crop, pl.ds(base + FIRST_DILATION, ROWS), :]
    upper = jnp.concatenate([cells, jnp.zeros((ROWS, 120), jnp.float32)], axis=1)
    upper = jnp.where(inside, pltpu.roll(upper, 124, axis=1), 0.0)
    z_upper = jnp.where(inside, growth * upper + pltpu.roll(outputs, 125, axis=1), 0.0)
    scale = scale_ref[0]
    grad_z = scale * z_upper
    grad_upper = grad_z * growth
    mixed_ref[...] = grad_upper[:, :8]
    grad_log = jnp.where(inside, grad_upper * upper - scale, 0.0)
    grad_outputs = grad_log + pltpu.roll(grad_z, 3, axis=1)
    grad_skip = grad_outputs[:, 0:1] * end_ref[0:1, :]
    for j in range(1, 6):
        grad_skip = grad_skip + grad_outputs[:, j : j + 1] * end_ref[j : j + 1, :]
    grad_skip = grad_skip.astype(jnp.bfloat16)
    grads_ref[...] = grad_skip
    grad_gated = dot_as(DNT, grad_skip, out_ref[2])
    grad_left = (grad_gated * (1.0 - tangent * tangent) * part).astype(jnp.bfloat16)
    grad_right = (grad_gated * tangent * part * (1.0 - part)).astype(jnp.bfloat16)
    low_ref[:, :H] = grad_left
    low_ref[:, H:] = grad_right
    sums_ref[0:8] += _three(DTN, _split(grad_outputs), halves_total)[0:8]
    sums_ref[8:9] += jnp.sum(grad_left.astype(jnp.float32), axis=0, keepdims=True)
    sums_ref[9:10] += jnp.sum(grad_right.astype(jnp.float32), axis=0, keepdims=True)
    sums_ref[10:11] += jnp.sum(grad_skip.astype(jnp.float32), axis=0, keepdims=True)
    sums_ref[11:12, :128] += jnp.sum(grad_outputs, axis=0, keepdims=True)
    sums_ref[12:13, :128] += jnp.sum(0.5 * z_upper * z_upper - log_scale, axis=0, keepdims=True)


def third_kernel(
    place_ref, own_ref, before_halo, after_halo, grads_ref, before_ref, out_ref, w0, w1, w2, w3,
    hidden_ref, residual_ref, low_ref, sums_ref, taps_ref, wide_ref, sem,
):
    step = pl.program_id(0)
    sources = (w0, w1, w2, w3)
    crops, length = own_ref.shape[:2]
    margin = 2 * FIRST_DILATION

    @pl.when(step == 0)
    def _():
        fetch_taps(place_ref, sources, taps_ref, sem, 1)
        wide_ref[:, :margin] = before_halo[...]
        wide_ref[:, margin : margin + length] = own_ref[...]
        wide_ref[:, margin + length :] = after_halo[...]
        sums_ref[...] = jnp.zeros_like(sums_ref)
        await_taps(sources, taps_ref, sem)

    per_crop = length // ROWS
    crop = step // per_crop
    base = pl.multiple_of((step % per_crop) * ROWS, ROWS)
    total = None
    for k in range(3):
        for half in range(2):
            window = wide_ref[crop, pl.ds(base + margin * (2 - k), ROWS), H * half : H * half + H]
            part = dot_as(DNT, window, taps_ref[2 * k + half])
            total = part if total is None else total + part
    hidden_ref[...] = total
    residual = total.astype(jnp.bfloat16)
    residual_ref[...] = residual
    grad_gated = dot_as(DNT, grads_ref[...], out_ref[1]) + dot_as(DNT, residual, out_ref[0])
    tangent, part = jnp.tanh(before_ref[:, :H]), sigmoid(before_ref[:, H:])
    grad_left = (grad_gated * (1.0 - tangent * tangent) * part).astype(jnp.bfloat16)
    grad_right = (grad_gated * tangent * part * (1.0 - part)).astype(jnp.bfloat16)
    low_ref[:, :H] = grad_left
    low_ref[:, H:] = grad_right
    sums_ref[0:1] += jnp.sum(residual.astype(jnp.float32), axis=0, keepdims=True)
    sums_ref[1:2] += jnp.sum(grad_left.astype(jnp.float32), axis=0, keepdims=True)
    sums_ref[2:3] += jnp.sum(grad_right.astype(jnp.float32), axis=0, keepdims=True)


def taps_kernel(place_ref, *refs, layer, pieces, owned):
    inputs, low_ref = refs[:pieces], refs[pieces]
    outs = refs[-3 - 2 * owned : -3]
    wide_ref, buffer_ref, sem = refs[-3:]
    crops, length = low_ref.shape[:2]
    margin = FIRST_DILATION * 2**layer
    offset = 0
    for piece in inputs:
        width = piece.shape[1]
        for crop in range(crops):
            wide_ref[crop, offset : offset + width] = piece[crop]
        offset += width
    for k in range(3):
        for half in range(2):
            j = 2 * k + half
            total = None
            for crop in range(crops):
                window = wide_ref[crop, margin * k : margin * k + length]
                part = dot_as(DTN, window, low_ref[crop, :, H * half : H * half + H])
                total = part if total is None else total + part
            buffer_ref[j] = total.astype(jnp.bfloat16)
            place = place_ref[6 * layer + j]
            relation = place // owned
            target = (relation // 2) * owned + place % owned
            for d, out_ref in enumerate(outs):

                @pl.when(target == d)
                def _(out_ref=out_ref):
                    pltpu.make_async_copy(buffer_ref.at[j], out_ref.at[relation % 2], sem.at[j]).start()

    for j in range(6):
        pltpu.make_async_copy(buffer_ref.at[j], outs[0].at[0], sem.at[j]).wait()


def start_kernel(
    place_ref, low_ref, above_ref, cells_ref, aux_ref, w0, w1, w2, w3,
    start_ref, lower_ref, taps_ref, wide_ref, end_ref, sem,
):
    crop = pl.program_id(0)
    sources = (w0, w1, w2, w3)
    length = low_ref.shape[1]
    margin = FIRST_DILATION

    @pl.when(crop == 0)
    def _():
        fetch_taps(place_ref, sources, taps_ref, sem, 0)
        start_ref[...] = jnp.zeros_like(start_ref)
        end_ref[...] = jnp.zeros_like(end_ref)
        end_ref[0:3] = aux_ref[0:3, :]
        await_taps(sources, taps_ref, sem)

    wide_ref[...] = jnp.zeros_like(wide_ref)
    wide_ref[margin : margin + length] = above_ref[...]
    for k in range(3):
        flowing = dot_as(DNT, low_ref[0, :, :H], taps_ref[2 * k])
        flowing = flowing + dot_as(DNT, low_ref[0, :, H:], taps_ref[2 * k + 1])
        wide_ref[margin * k : margin * k + length] += flowing
    pieces = _split(wide_ref[...])
    cells = cells_ref[crop]
    cells = jnp.concatenate([cells, jnp.zeros((cells.shape[0], 120), jnp.float32)], axis=1)
    start_ref[...] += _three(DTN, _split(cells), pieces)[0:8]
    lower_ref[0] = _three(DNT, pieces, _split(end_ref[...]))[:, :8]


def smem():
    return pl.BlockSpec(memory_space=pltpu.SMEM)


def vmem():
    return pl.BlockSpec(memory_space=pltpu.VMEM)


def anywhere():
    return pl.BlockSpec(memory_space=pl.ANY)


def by_rows(width):
    return pl.BlockSpec((ROWS, width), lambda i: (i, 0))


def fixed(shape, index):
    return pl.BlockSpec(shape, lambda i: index)


def shaped(shape, dtype=jnp.float32):
    return jax.ShapeDtypeStruct(shape, dtype)


def taps_gradient(place, pieces, low, layer, owned, targets=()):
    crops, length = low.shape[:2]
    width = sum(piece.shape[1] for piece in pieces)
    return pl.pallas_call(
        lambda *refs: taps_kernel(*refs, layer=layer, pieces=len(pieces), owned=owned),
        out_shape=[shaped((2, H, H), jnp.bfloat16)] * (2 * owned),
        in_specs=[smem()] + [vmem() for _ in pieces] + [vmem()] + [anywhere() for _ in targets],
        out_specs=[anywhere()] * (2 * owned),
        scratch_shapes=[
            pltpu.VMEM((crops, width, H), jnp.bfloat16),
            pltpu.VMEM((6, H, H), jnp.bfloat16),
            pltpu.SemaphoreType.DMA((6,)),
        ],
        input_output_aliases={len(pieces) + 2 + i: i for i in range(len(targets))},
        name=f"taps_gradient_{layer}",
    )(place, *pieces, low, *targets)


def halo(cells, width):
    count = lax.axis_size("tm")
    head, tail = cells[:, :width], cells[:, cells.shape[1] - width :]
    return (
        lax.ppermute(tail, "tm", [(i, i + 1) for i in range(count - 1)]),
        lax.ppermute(head, "tm", [(i + 1, i) for i in range(count - 1)]),
    )


def gather_relative(values, axis, bits):
    for bit in bits:
        values = jnp.concatenate([values, swap(values, axis, bit)], axis=0)
    return values


def reduced_slot(kept, sent):
    other = yield sent, "opt", 1
    sent, kept = kept[1] + other[1], kept[0] + other[0]
    other = yield sent, "opt", 2
    part = kept.astype(jnp.float32) + other.astype(jnp.float32)
    bits = bits_of("tm")
    for bit in bits[:-1]:
        kept, sent = halves(part, "tm", bit, 0)
        other = yield sent.astype(jnp.bfloat16), "tm", bit
        part = kept + other.astype(jnp.float32)
    part = part.astype(jnp.bfloat16)
    other = yield part, "tm", bits[-1]
    part = part + other
    for bit in reversed(bits[:-1]):
        other = yield part, "tm", bit
        part = ordered(part, other, "tm", bit, 0)
    return part


def swap_all(values, axis, bit):
    return jax.tree.map(lambda value: swap(value, axis, bit), values)


def lowest_half(values, bit, dim):
    shape = values.shape
    values = values.reshape(*shape[:dim], shape[dim] // 2, 2, *shape[dim + 1 :])
    kept, sent = halves(values, "tm", bit, dim + 1)
    shape = (*shape[:dim], shape[dim] // 2, *shape[dim + 1 :])
    return kept.reshape(shape), sent.reshape(shape)


def wide(values):
    return jax.tree.map(lambda value: value.astype(jnp.float32), values)


def narrow(values):
    return jax.tree.map(lambda value: value.astype(jnp.bfloat16), values)


def spread_rest(cond, out, small):
    other = yield (cond[1], out[1], small), "opt", 1
    cond = [mine + theirs for mine, theirs in zip(cond[0], wide(other[0]))]
    out, small = out[0] + wide(other[1]), small + other[2]
    width = cond[0].shape[0] // 2
    other = yield (narrow([part[width:] for part in cond]), narrow(out[1]), small), "opt", 2
    cond = [mine[:width] + theirs for mine, theirs in zip(cond, wide(other[0]))]
    out, small = out[0] + wide(other[1]), small + other[2]
    count = lax.axis_size("tm")
    cond = jnp.concatenate(cond, axis=1).reshape(width, count, -1)
    cond = jnp.swapaxes(cond, 0, 1)
    out = out.reshape(out.shape[0], count, -1, out.shape[2])
    for bit in bits_of("tm"):
        cond, sent = lowest_half(cond, bit, 0)
        out, sent_out = lowest_half(out, bit, 1)
        other = yield (narrow(sent), narrow(sent_out), small), "tm", bit
        cond, out, small = cond + wide(other[0]), out + wide(other[1]), small + other[2]
    return cond[0].T, out[:, 0], small


def reduce_slots(keep, send, work, follow, entry):
    waiting = [reduced_slot(kept, sent) for kept, sent in zip(keep, send)]
    owned = len(keep)
    requests, done, results, latest = {}, {}, [], ()
    slot = 0
    while len(done) < owned:
        if slot < owned:
            requests[slot] = next(waiting[slot])
        if slot == entry:
            waiting.append(follow(results + [latest]))
            requests[owned] = next(waiting[owned])
        held = {i: r for i, r in requests.items() if i == owned and r[1] == "tm"}
        active = sorted(set(requests) - set(held))
        task, inputs = work.get(slot, (None, ()))
        values, inputs, latest = lax.optimization_barrier(
            (tuple(requests[i][0] for i in active), inputs, latest)
        )
        if slot - 1 in work:
            results.append(latest)
        answers = [swap_all(value, *requests[i][1:]) for value, i in zip(values, active)]
        latest = () if task is None else task(*inputs)
        requests = held
        for answer, i in zip(answers, active):
            try:
                requests[i] = waiting[i].send(answer)
            except StopIteration as stop:
                done[i] = stop.value
        slot += 1
    total = jnp.stack([done[i] for i in range(owned)])
    value, *where = requests[owned]
    value, total = lax.optimization_barrier((value, total))
    while True:
        try:
            value, *where = waiting[owned].send(swap_all(value, *where))
        except StopIteration as stop:
            return total, stop.value


def adamw_update(weight, gradient, moment_one, moment_two, steps_done, rate_value):
    moment_one = beta_first * moment_one + (1.0 - beta_first) * gradient
    moment_two = beta_second * moment_two + (1.0 - beta_second) * gradient * gradient
    direction = (
        moment_one
        / (1.0 - beta_first**steps_done)
        / (jnp.sqrt(moment_two / (1.0 - beta_second**steps_done)) + epsilon)
    )
    weight = weight - rate_value * (direction + decay_weight * weight)
    return (weight, moment_one, moment_two)


def shards(
    wave,
    crop_offsets,
    squeeze_order,
    mel,
    mel_index,
    soap_slots,
    step_count,
    in_weight,
    soap_first,
    soap_second,
    left_stats,
    right_stats,
    left_basis,
    right_basis,
    cond_weight,
    cond_first,
    cond_second,
    out_weight,
    out_first,
    out_second,
    aux_params,
    aux_first,
    aux_second,
    flow_params,
    flow_first,
    flow_second,
):
    crops_current = wave.shape[0]
    row_count = crops_current * G_DEV
    tokens_all = row_count * lax.axis_size("tm") * lax.axis_size("opt")
    scale_final = 1.0 / (6.0 * tokens_all)
    scale_early = early_weight / (2.0 * tokens_all)
    steps_done = step_count[0].astype(jnp.float32)
    owned = in_weight.shape[0]
    rank = lax.axis_index("opt")
    own = in_weight.astype(jnp.bfloat16)
    cond_part = cond_weight.astype(jnp.bfloat16).T
    out_part = out_weight.astype(jnp.bfloat16)[None]
    own, cond_part, out_part = lax.optimization_barrier((own, cond_part, out_part))
    cond_across, out_across = swap(cond_part, "opt", 2), swap(out_part, "opt", 2)
    own, cond_part, cond_across, out_part, out_across, wave, mel_index = lax.optimization_barrier(
        (own, cond_part, cond_across, out_part, out_across, wave, mel_index)
    )
    tm_rank, tm_bits = lax.axis_index("tm"), bits_of("tm")[::-1]
    count_tm = lax.axis_size("tm")
    segments = [
        lax.dynamic_slice_in_dim(wave[crop, 0], crop_offsets[crop], 8 * G_DEV, 0).reshape(G_DEV, 8)
        for crop in range(crops_current)
    ]
    chosen = jnp.arange(8, dtype=jnp.int32)[:, None] == squeeze_order[None, :]
    squeezed = full_dot(jnp.concatenate(segments), chosen.astype(jnp.float32))
    squeezed = squeezed.reshape(crops_current, G_DEV, 8)
    flow_matrix = flow_params[:, :6]
    mixed = full_dot(squeezed.reshape(row_count, 8)[:, 2:], flow_matrix.T)
    lower_half, upper_half = mixed[:, :3], mixed[:, 3:]
    cells = jnp.concatenate(
        [
            lower_half,
            jnp.ones((row_count, 1), jnp.float32),
            upper_half,
            jnp.zeros((row_count, 1), jnp.float32),
        ],
        axis=1,
    ).reshape(crops_current, G_DEV, 8)
    edge = jnp.concatenate([cells, squeezed], axis=2)
    edge_before, edge_after = halo(edge, FIRST_DILATION)
    edge = jnp.concatenate([edge_before, edge, edge_after], axis=1)
    cells_wide, squeezed_wide = edge[..., :8], edge[..., 8:]

    slots = jnp.arange(NMAT, dtype=jnp.int32)
    slot_of = jnp.sum(
        jnp.where(soap_slots[None, :] == slots[:, None], slots[None, :], 0), axis=1
    ).astype(jnp.int32)
    relation = (slot_of // owned) ^ rank
    place = ((relation % 2) * 2 + relation // 2) * owned + slot_of % owned

    spots = jnp.zeros((count_tm,), jnp.int32)
    for index, bit in enumerate(tm_bits):
        distance = jnp.arange(count_tm, dtype=jnp.int32) ^ tm_rank
        spots = spots + ((distance // bit) % 2) * (1 << index)
    columns = rank ^ jnp.array([0, 2, 1, 3], jnp.int32)

    across = swap(own, "opt", 2)
    cond_part = jnp.concatenate([cond_part, cond_across], axis=0)[None]
    out_part = jnp.concatenate([out_part, out_across], axis=0)[None]
    own_core = swap(own, "opt", 1)
    across_core = swap(across, "opt", 1)
    sources = (own, across, own_core, across_core)
    cond_part = gather_relative(cond_part, "tm", tm_bits)
    out_part = gather_relative(out_part, "tm", tm_bits)
    if count_tm != 8:
        fold = count_tm // 8
        cond_part = jnp.take(cond_part, spots, axis=0)
        cond_part = cond_part.reshape(8, fold, *cond_part.shape[1:])
        cond_part = jnp.moveaxis(cond_part, 1, 2).reshape(8, cond_part.shape[2], -1)
        out_part = jnp.take(out_part, spots, axis=0)
        out_part = out_part.reshape(8, fold, *out_part.shape[1:])
        out_part = jnp.moveaxis(out_part, 1, 3).reshape(8, 2, 3, 64, -1)
        spots = jnp.arange(8, dtype=jnp.int32)
    place = jnp.concatenate([place, spots, columns])

    spot_of = jnp.arange(2 * 4 * FR_DEV, dtype=jnp.int32)
    quarter = (spot_of // FR_DEV) % 4
    sample = 2 * (rank ^ (spot_of // (4 * FR_DEV)) ^ (2 * (quarter // 2))) + quarter % 2
    spread = (jnp.arange(8, dtype=jnp.int32)[:, None] == sample[None, :]).astype(jnp.bfloat16)
    frames = half_dot(mel_index.reshape(row_count, 8).astype(jnp.bfloat16), spread)
    hits = (frames == (spot_of % FR_DEV).astype(jnp.float32)[None, :]).astype(jnp.bfloat16)
    hits = hits.reshape(crops_current, G_DEV, 2, 4 * FR_DEV)
    same = jnp.eye(4, dtype=jnp.bfloat16)
    frame_blocks = (same[None, :, None, :, None] * mel[:, None, :, None, :]).reshape(
        crops_current, 4 * FR_DEV, 4 * MEL
    )
    cond_rows = tuple(
        jnp.einsum(
            "cgk,ckm->cgm", hits[:, :, side], frame_blocks, preferred_element_type=jnp.float32
        )
        .astype(jnp.bfloat16)
        .reshape(row_count, 4 * MEL)
        for side in (0, 1)
    )
    cond_part, out_part, cond_rows, cells_wide, squeezed_wide, place = lax.optimization_barrier(
        (cond_part, out_part, cond_rows, cells_wide, squeezed_wide, place)
    )
    cond_other = swap(cond_part, "opt", 1)
    out_other = swap(out_part, "opt", 1)
    steps = row_count // ROWS
    taps_scratch = [pltpu.VMEM((6, H, H), jnp.bfloat16)]
    sems = [pltpu.SemaphoreType.DMA((6,))]
    half_cols = 4 * MEL
    wide_rows = G_DEV + 2 * FIRST_DILATION
    before_first, gated_first, hidden_low, start_low, out_full = pl.pallas_call(
        first_kernel,
        grid=(steps,),
        out_shape=[
            shaped((row_count, 2 * H)),
            shaped((row_count, H), jnp.bfloat16),
            shaped((row_count, H), jnp.bfloat16),
            shaped((crops_current, wide_rows, H), jnp.bfloat16),
            shaped((3, H, H), jnp.bfloat16),
        ],
        in_specs=[smem(), vmem(), vmem(), by_rows(half_cols), by_rows(half_cols)]
        + [vmem()] * 4
        + [anywhere()] * 4,
        out_specs=[by_rows(2 * H), by_rows(H), by_rows(H), vmem(), vmem()],
        scratch_shapes=taps_scratch + sems,
        name="first_layer",
    )(
        place,
        cells_wide,
        aux_params,
        *cond_rows,
        cond_part,
        cond_other,
        out_part,
        out_other,
        *sources,
    )

    hidden_low = hidden_low.reshape(crops_current, G_DEV, H)
    margin = 2 * FIRST_DILATION
    hidden_halo = halo(hidden_low, margin)
    gated_second, grad_skip, low_second, grad_upper, sums_second = pl.pallas_call(
        second_kernel,
        grid=(steps,),
        out_shape=[
            shaped((row_count, H), jnp.bfloat16),
            shaped((row_count, H), jnp.bfloat16),
            shaped((row_count, 2 * H), jnp.bfloat16),
            shaped((row_count, 8)),
            shaped((16, H)),
        ],
        in_specs=[smem(), smem(), smem(), vmem(), vmem(), vmem(), vmem(), vmem()]
        + [by_rows(half_cols)] * 2
        + [vmem()] * 2
        + [by_rows(H), vmem()]
        + [anywhere()] * 4,
        out_specs=[by_rows(H), by_rows(H), by_rows(2 * H), by_rows(8), vmem()],
        scratch_shapes=taps_scratch
        + [pltpu.VMEM((crops_current, G_DEV + 2 * margin, H), jnp.bfloat16)]
        + [pltpu.VMEM((128, H), jnp.float32)]
        + sems,
        name="second_layer",
    )(
        place,
        jnp.full((1,), scale_final, jnp.float32),
        flow_params,
        hidden_low,
        *hidden_halo,
        aux_params,
        cells_wide,
        *cond_rows,
        cond_part,
        cond_other,
        gated_first,
        out_full,
        *sources,
    )
    low_cells = low_second.reshape(crops_current, G_DEV, 2 * H)
    low_halo = halo(low_cells, margin)
    grad_slots = taps_gradient(
        place, (hidden_halo[0], hidden_low, hidden_halo[1]), low_cells, 1, owned
    )
    grad_hidden, grad_residual, low_first, sums_first = pl.pallas_call(
        third_kernel,
        grid=(steps,),
        out_shape=[
            shaped((row_count, H)),
            shaped((row_count, H), jnp.bfloat16),
            shaped((row_count, 2 * H), jnp.bfloat16),
            shaped((8, H)),
        ],
        in_specs=[smem(), vmem(), vmem(), vmem(), by_rows(H), by_rows(2 * H), vmem()]
        + [anywhere()] * 4,
        out_specs=[by_rows(H), by_rows(H), by_rows(2 * H), vmem()],
        scratch_shapes=taps_scratch
        + [pltpu.VMEM((crops_current, G_DEV + 2 * margin, 2 * H), jnp.bfloat16)]
        + sems,
        name="first_gradient",
    )(place, low_cells, *low_halo, grad_skip, before_first, out_full, *sources)
    low_first_cells = low_first.reshape(crops_current, G_DEV, 2 * H)
    grad_slots = taps_gradient(place, (start_low,), low_first_cells, 0, owned, grad_slots)
    def start_work(low, above, cells):
        start, lower = pl.pallas_call(
            start_kernel,
            grid=(crops_current,),
            out_shape=[shaped((8, H)), shaped((crops_current, wide_rows, 8))],
            in_specs=[
                smem(),
                pl.BlockSpec((1, G_DEV, 2 * H), lambda i: (i, 0, 0)),
                pl.BlockSpec((G_DEV, H), lambda i: (i, 0)),
                vmem(),
                vmem(),
            ]
            + [anywhere()] * 4,
            out_specs=[vmem(), pl.BlockSpec((1, wide_rows, 8), lambda i: (i, 0, 0))],
            scratch_shapes=taps_scratch
            + [pltpu.VMEM((wide_rows, H), jnp.float32), pltpu.VMEM((128, H), jnp.float32)]
            + sems,
            name="start_gradient",
        )(place, low, above, cells, aux_params, *sources)
        return (start[:4], lower.reshape(-1, 8)[:, :3])

    def cond_work(own_rows, other_rows, first, second):
        return tuple(
            tuple(rows_dot(rows, low).astype(kind) for low in (first, second))
            for rows, kind in ((own_rows, jnp.float32), (other_rows, jnp.bfloat16))
        )

    def out_work(first, second, above, skip):
        pairs = ((first, above), (first, skip), (second, skip))
        grads = jnp.stack([rows_dot(*pair) for pair in pairs])
        return tuple(
            jnp.stack(
                [
                    lax.dynamic_slice_in_dim(grads, (rank ^ core ^ bit) * 128, 128, 2)
                    for bit in (0, 2)
                ]
            )
            for core in (0, 1)
        )

    def out_parts(*inputs):
        own, other = out_work(*inputs)
        return own, other.astype(jnp.bfloat16)

    def rest_of(results):
        (grad_start, grad_lower), grad_cond, grad_out = results
        final_part = jnp.sum(sums_second[12]) + 0.5 * jnp.sum(lower_half * lower_half)
        early_part = 0.5 * jnp.sum(squeezed[..., :2] * squeezed[..., :2])
        flow_lower = rows_dot(grad_lower, squeezed_wide.reshape(-1, 8)[:, 2:], highest)
        flow_lower = flow_lower + scale_final * rows_dot(
            lower_half, squeezed.reshape(-1, 8)[:, 2:], highest
        )
        flow_upper = rows_dot(grad_upper[:, :3], squeezed.reshape(-1, 8)[:, 2:], highest)
        grad_flow = jnp.concatenate(
            [jnp.concatenate([flow_lower, flow_upper], axis=0), sums_second[11, :6][:, None]], axis=1
        )
        grad_aux = jnp.concatenate(
            [
                grad_start,
                sums_first[1:3],
                sums_second[8:10],
                sums_first[0:1],
                sums_second[10:11],
                sums_second[10:11],
                sums_second[0:6],
            ],
            axis=0,
        )
        small = jnp.concatenate(
            [grad_aux.reshape(-1), grad_flow.reshape(-1), jnp.stack([final_part, early_part])]
        )
        small = jnp.pad(small, (0, -small.shape[0] % 1024)).reshape(-1, 128)
        return spread_rest(grad_cond, grad_out, small)

    grad_owned, (grad_cond, grad_out, small) = reduce_slots(
        grad_slots[:owned],
        grad_slots[owned:],
        {
            1: (start_work, (low_first_cells, grad_hidden, cells_wide)),
            2: (cond_work, (*cond_rows, low_first, low_second)),
            3: (out_parts, (gated_first, gated_second, grad_residual, grad_skip)),
        },
        rest_of,
        4,
    )
    grad_owned = grad_owned.astype(jnp.float32)
    small = small.reshape(-1)
    filled = aux_params.size + flow_params.size + 2
    grad_aux = small[: aux_params.size].reshape(aux_params.shape)
    grad_flow = small[aux_params.size : filled - 2].reshape(flow_params.shape)
    parts = small[filled - 2 : filled]
    factor = jnp.linalg.cholesky(full_dot(flow_matrix, flow_matrix.T))
    log_det = jnp.sum(jnp.log(jnp.diagonal(factor)))
    inverse_t = jax.scipy.linalg.cho_solve((factor, True), flow_matrix)
    grad_flow = grad_flow.at[:, :6].add(-inverse_t / 6.0)
    loss = parts[0] * scale_final + parts[1] * scale_early - log_det / 6.0
    (
        in_new,
        soap_first_new,
        soap_second_new,
        left_stats_new,
        right_stats_new,
        left_basis_new,
        right_basis_new,
        (grad_cond, grad_out),
    ) = soap_update(
        in_weight,
        grad_owned,
        soap_first,
        soap_second,
        left_stats,
        right_stats,
        left_basis,
        right_basis,
        steps_done,
        (grad_cond, grad_out),
    )
    cond_new, cond_first_new, cond_second_new = adamw_update(
        cond_weight, grad_cond, cond_first, cond_second, steps_done, learn_rate
    )
    out_new, out_first_new, out_second_new = adamw_update(
        out_weight, grad_out, out_first, out_second, steps_done, learn_rate
    )
    aux_new, aux_first_new, aux_second_new = adamw_update(
        aux_params, grad_aux, aux_first, aux_second, steps_done, aux_rate
    )
    flow_new, flow_first_new, flow_second_new = adamw_update(
        flow_params, grad_flow, flow_first, flow_second, steps_done, learn_rate
    )
    return (
        loss,
        in_new,
        soap_first_new,
        soap_second_new,
        left_stats_new,
        right_stats_new,
        left_basis_new,
        right_basis_new,
        cond_new,
        cond_first_new,
        cond_second_new,
        out_new,
        out_first_new,
        out_second_new,
        aux_new,
        aux_first_new,
        aux_second_new,
        flow_new,
        flow_first_new,
        flow_second_new,
    )


def solution(mesh):
    placed = (
        P("opt", "tm", None),
        P("opt"),
        P(),
        P("opt", "tm", None),
        P("opt", "tm", None),
        P(),
        P(),
        P("opt", None, None),
        P("opt", None, None),
        P("opt", None, None),
        P("opt", None, None),
        P("opt", None, None),
        P("opt", None, None),
        P("opt", None, None),
        P("tm", "opt"),
        P("tm", "opt"),
        P("tm", "opt"),
        P(None, "tm", "opt"),
        P(None, "tm", "opt"),
        P(None, "tm", "opt"),
        P(),
        P(),
        P(),
        P(),
        P(),
        P(),
    )
    return jax.shard_map(
        shards,
        mesh=mesh,
        in_specs=placed,
        out_specs=(
            P(),
            P("opt", None, None),
            P("opt", None, None),
            P("opt", None, None),
            P("opt", None, None),
            P("opt", None, None),
            P("opt", None, None),
            P("opt", None, None),
            P("tm", "opt"),
            P("tm", "opt"),
            P("tm", "opt"),
            P(None, "tm", "opt"),
            P(None, "tm", "opt"),
            P(None, "tm", "opt"),
            P(),
            P(),
            P(),
            P(),
            P(),
            P(),
        ),
        check_vma=False,
    )
```

```python
import jax
import jax.numpy as jnp
from jax import lax
from jax.experimental import pallas as pl
from jax.experimental.pallas import tpu as pltpu
from jax.sharding import PartitionSpec as P

H = 512
MEL = 80
LAYERS = 2
FIRST_DILATION = 64
G_DEV = 512
FR_DEV = 16
NMAT = 12


highest = lax.Precision.HIGHEST
beta_first = 0.9
beta_second = 0.99
beta_stats = 0.95
learn_rate = 0.02
aux_rate = 0.15
epsilon = 1e-08
decay_weight = 0.01
early_weight = 0.5


def full_dot(matrix_a, matrix_b):
    return jnp.dot(matrix_a, matrix_b, precision=highest, preferred_element_type=jnp.float32)


def half_dot(matrix_a, matrix_b):
    return jnp.dot(matrix_a, matrix_b, preferred_element_type=jnp.float32)


def rows_dot(matrix_a, matrix_b, exactness=None):
    return lax.dot_general(
        matrix_a,
        matrix_b,
        (((0,), (0,)), ((), ())),
        precision=exactness,
        preferred_element_type=jnp.float32,
    )


def cols_dot(matrix_a, matrix_b):
    return lax.dot_general(
        matrix_a, matrix_b, (((1,), (1,)), ((), ())), preferred_element_type=jnp.float32
    )


PIVOTS = 8


def _nt(x, y):
    return _three(NT, _split(x), _split(y))


def _nn(x, y):
    return _three(NN, _split(x), _split(y))


def _split(x):
    hi = x.astype(jnp.bfloat16)
    return hi, (x - hi.astype(jnp.float32)).astype(jnp.bfloat16)

def _three(dims, x, y):
    xh, xl = x
    yh, yl = y
    dot = lambda a, b: lax.dot_general(a, b, dims, preferred_element_type=jnp.float32)
    return dot(xh, yh) + (dot(xh, yl) + dot(xl, yh))

NT = (((1,), (1,)), ((), ()))
NN = (((1,), (0,)), ((), ()))

def pair_inverse(blocks):
    lane = lax.broadcasted_iota(jnp.int32, (8, 128), 1)
    sub = lax.broadcasted_iota(jnp.int32, (8, 128), 0)
    local = lane % 64
    half = lane - local
    groups = [[block[8 * g:8 * g + 8] for g in range(8)] for block in blocks]
    for start in range(0, 64, PIVOTS):
        first, low = divmod(start, 8)
        inside = (local >= start) & (local < start + PIVOTS)
        for rows in groups:
            cols = []
            for n in range(PIVOTS):
                pick = half + (start + n)
                cols.append([jnp.take_along_axis(rows[g], pick, axis=1, mode="promise_in_bounds") for g in range(first, 8)])
            lead = rows[first]
            entry = [[cols[n][0][low + m:low + m + 1] for n in range(m + 1)] for m in range(PIVOTS)]
            work = [jnp.where(local == start + m, 1.0, jnp.where(inside, 0.0, jnp.broadcast_to(lead[low + m:low + m + 1], (8, 128)))) for m in range(PIVOTS)]
            entry = [[jnp.broadcast_to(e, (8, 128)) for e in line] for line in entry]
            scaled = []
            ratio = {}
            for m in range(PIVOTS):
                inverse = 1.0 / entry[m][m]
                for n in range(m + 1, PIVOTS):
                    ratio[n, m] = entry[n][m] * inverse
                for n in range(m + 1, PIVOTS):
                    work[n] = work[n] - ratio[n, m] * work[m]
                    for q in range(m + 1, n + 1):
                        entry[n][q] = entry[n][q] - ratio[n, m] * entry[q][m]
                scaled.append(work[m] * inverse)
            final = [work[m] * lax.rsqrt(entry[m][m]) for m in range(PIVOTS)]
            for m in range(PIVOTS - 2, -1, -1):
                for n in range(m + 1, PIVOTS):
                    scaled[m] = scaled[m] - ratio[n, m] * scaled[n]
            for g in range(first, 8):
                old = jnp.where(inside, 0.0, rows[g])
                new = old
                for n in range(PIVOTS):
                    new = new - cols[n][g - first] * scaled[n]
                if g == first:
                    kept = rows[g]
                    for m in range(PIVOTS):
                        kept = jnp.where(sub == low + m, final[m], kept)
                    new = jnp.where(sub >= low + PIVOTS, new, kept)
                rows[g] = new
    return [
        jnp.concatenate([jnp.where(local <= 8 * g + sub, rows[g], 0.0) for g in range(8)], axis=0)
        for rows in groups
    ]

def beside(x, y):
    return jnp.concatenate([x, y], axis=1)

def paired(block):
    wide = jnp.concatenate([block, block], axis=0)
    row = lax.broadcasted_iota(jnp.int32, (128, 128), 0)
    col = lax.broadcasted_iota(jnp.int32, (128, 128), 1)
    return jnp.where((row // 64) == (col // 64), wide, 0.0)

def factor_kernel(
    gram_left, gram_right, tall_left, tall_right, out_left, out_right, s_ref, a_ref, y_ref, l_ref, w_ref
):
    owned = gram_left.shape[0]
    count = 2 * owned
    outs = [out_left.at[i] for i in range(owned)] + [out_right.at[i] for i in range(owned)]
    step = pl.program_id(0)

    @pl.when(step == 0)
    def _():
        s_ref[:owned] = gram_left[...]
        s_ref[owned:] = gram_right[...]
        a_ref[:owned] = tall_left[...]
        a_ref[owned:] = tall_right[...]

    start = pl.multiple_of(step * 128, 128)
    diag = [s_ref[i, pl.ds(start, 128), pl.ds(start, 128)] for i in range(count)]
    pairs = range(count // 2)
    top = pair_inverse([beside(diag[2 * p][:64, :64], diag[2 * p + 1][:64, :64]) for p in pairs])
    cross, below = [], []
    for p in pairs:
        low = beside(diag[2 * p][64:, :64], diag[2 * p + 1][64:, :64])
        factor = _nt(low, paired(top[p]))
        cross.append(factor)
        rest = beside(diag[2 * p][64:, 64:], diag[2 * p + 1][64:, 64:])
        below.append(rest - _nt(factor, paired(factor)))
    bottom = pair_inverse(below)
    for p in pairs:
        corner = -_nn(_nn(bottom[p], paired(cross[p])), paired(top[p]))
        zero = jnp.zeros((64, 64), jnp.float32)
        for side in range(2):
            cut = slice(64 * side, 64 * side + 64)
            w_ref[2 * p + side, :64] = beside(top[p][:, cut], zero)
            w_ref[2 * p + side, 64:] = beside(corner[:, cut], bottom[p][:, cut])

    @pl.when(step % 2 == 0)
    def _():
        for i in range(count):
            inv = w_ref[i]
            y_ref[i, :128, :128] = inv
            y_ref[i, :128, 128:] = jnp.zeros((128, 128), jnp.float32)
            low = s_ref[i, pl.ds(start + 128, 128), pl.ds(start, 128)]
            factor = _nt(low, inv)
            l_ref[i] = factor
            s_ref[i, pl.ds(start + 128, 128), pl.ds(start + 128, 128)] -= _nt(factor, factor)

    @pl.when(step % 2 == 1)
    def _():
        for i in range(count):
            inv = w_ref[i]
            y_ref[i, 128:, :128] = -_nn(_nn(inv, l_ref[i]), y_ref[i, :128, :128])
            y_ref[i, 128:, 128:] = inv

    @pl.when(step == 1)
    def _():
        for i in range(count):
            inv = y_ref[i]
            factor = _nt(s_ref[i, 256:, :256], inv)
            s_ref[i, 256:, 256:] -= _nt(factor, factor)
            inv = _split(inv)
            done = _three(NT, _split(a_ref[i, :, :256]), inv)
            outs[i][:, :256] = done
            a_ref[i, :, 256:] -= _three(NT, _split(done), _split(factor))

    @pl.when(step == 3)
    def _():
        for i in range(count):
            outs[i][:, 256:] = _three(NT, _split(a_ref[i, :, 256:]), _split(y_ref[i]))

def orthonormal_all(grams, talls):
    count = 2 * grams[0].shape[0]
    whole = lambda: pl.BlockSpec(memory_space=pltpu.VMEM)
    return pl.pallas_call(
        factor_kernel,
        grid=(4,),
        out_shape=[jax.ShapeDtypeStruct(tall.shape, jnp.float32) for tall in talls],
        in_specs=[whole() for _ in range(4)],
        out_specs=[whole(), whole()],
        scratch_shapes=[
            pltpu.VMEM((count, 512, 512), jnp.float32),
            pltpu.VMEM((count, 512, 512), jnp.float32),
            pltpu.VMEM((count, 256, 256), jnp.float32),
            pltpu.VMEM((count, 128, 128), jnp.float32),
            pltpu.VMEM((count, 128, 128), jnp.float32),
        ],
        name="orthonormal",
    )(*grams, *talls)


def high_dot(matrix_a, matrix_b, dims):
    return lax.dot_general(
        matrix_a, matrix_b, dims, precision=lax.Precision.HIGH, preferred_element_type=jnp.float32
    )


def low_dot(matrix_a, matrix_b, dims):
    return lax.dot_general(
        matrix_a.astype(jnp.bfloat16),
        matrix_b.astype(jnp.bfloat16),
        dims,
        preferred_element_type=jnp.float32,
    )


PLAIN = (((2,), (1,)), ((0,), (0,)))
FIRST = (((1,), (1,)), ((0,), (0,)))
SECOND = (((2,), (2,)), ((0,), (0,)))


def soap_update(
    weight,
    gradient,
    moment_one,
    moment_two,
    left_stats,
    right_stats,
    left_basis,
    right_basis,
    steps_done,
    rest,
):
    owned = weight.shape[0]
    turned = high_dot(left_basis, gradient.astype(jnp.float32), FIRST)
    rotated = high_dot(turned, right_basis, PLAIN)
    moment_one = beta_first * moment_one + (1.0 - beta_first) * rotated
    moment_two = beta_second * moment_two + (1.0 - beta_second) * rotated * rotated
    direction = (
        moment_one
        / (1.0 - beta_first**steps_done)
        / (jnp.sqrt(moment_two / (1.0 - beta_second**steps_done)) + epsilon)
    )
    direction = lax.optimization_barrier(direction.astype(jnp.bfloat16))
    weight = weight - learn_rate * (
        low_dot(low_dot(left_basis, direction, PLAIN), right_basis, SECOND) + decay_weight * weight
    )
    left_stats = beta_stats * left_stats + (1.0 - beta_stats) * low_dot(gradient, gradient, SECOND)
    right_stats = beta_stats * right_stats + (1.0 - beta_stats) * low_dot(gradient, gradient, FIRST)
    talls = (high_dot(left_stats, left_basis, PLAIN), high_dot(right_stats, right_basis, PLAIN))
    talls = advance(rest, talls)
    grams = tuple(high_dot(tall, tall, FIRST) for tall in talls)
    grams = advance(rest, grams)
    left_new, right_new = orthonormal_all(grams, talls)
    initial = high_dot(high_dot(left_basis, moment_one, PLAIN), right_basis, SECOND)
    moment_one = high_dot(high_dot(left_new, initial, FIRST), right_new, PLAIN)
    return (weight, moment_one, moment_two, left_stats, right_stats, left_new, right_new)


def swap(values, axis, bit):
    return lax.ppermute(values, axis, [(i, i ^ bit) for i in range(lax.axis_size(axis))])


def side_of(axis, bit):
    return (lax.axis_index(axis) // bit) % 2


def ordered(values, others, axis, bit, dim):
    first = side_of(axis, bit) == 0
    return jnp.concatenate(
        [jnp.where(first, values, others), jnp.where(first, others, values)], axis=dim
    )


def halves(values, axis, bit, dim):
    width = values.shape[dim] // 2
    side = side_of(axis, bit)
    return (
        lax.dynamic_slice_in_dim(values, side * width, width, dim),
        lax.dynamic_slice_in_dim(values, (1 - side) * width, width, dim),
    )


def bits_of(axis):
    count = lax.axis_size(axis)
    return [1 << i for i in range(count.bit_length() - 1)]


def scatter_half(values, axis, bit, dim):
    kept, sent = halves(values, axis, bit, dim)
    return kept + swap(sent, axis, bit)


def all_sum(values):
    for axis in ("opt", "tm"):
        for bit in bits_of(axis):
            values = values + swap(values, axis, bit)
    return values


def gather_blocks(values, axis, bits):
    for bit in bits:
        values = ordered(values, swap(values, axis, bit), axis, bit, 0)
    return values


ROWS = 256
DNT = (((1,), (1,)), ((), ()))
DTN = (((0,), (0,)), ((), ()))


def dot_as(dims, x, y):
    return lax.dot_general(x, y, dims, preferred_element_type=jnp.float32)


def fetch_taps(place_ref, sources, taps_ref, sem, layer):
    owned = sources[0].shape[0]
    for j in range(6):
        place = place_ref[6 * layer + j]
        for r, source in enumerate(sources):

            @pl.when(place // owned == r)
            def _(source=source):
                pltpu.make_async_copy(source.at[place % owned], taps_ref.at[j], sem.at[j]).start()


def await_taps(sources, taps_ref, sem):
    for j in range(6):
        pltpu.make_async_copy(sources[0].at[0], taps_ref.at[j], sem.at[j]).wait()


def sigmoid(x):
    return 0.5 * jnp.tanh(0.5 * x) + 0.5


def gate_inputs(
    layer, info_ref, cond_refs, weight_refs, aux_ref, crop_ref, crop, base, dilation, taps_ref
):
    sums = []
    for half in range(2):
        parts = []
        for block in range(2):
            spot = info_ref[NMAT + 4 * layer + 2 * half + block]
            part = dot_as(NN, cond_refs[0][...], weight_refs[0][spot])
            parts.append(part + dot_as(NN, cond_refs[1][...], weight_refs[1][spot]))
        total = jnp.concatenate(parts, axis=1) + aux_ref[4 + 2 * layer + half : 5 + 2 * layer + half, :]
        for k in range(3):
            window = crop_ref[crop, pl.ds(base + dilation * k, ROWS), :]
            total = total + dot_as(NN, window, taps_ref[2 * k + half])
        sums.append(total)
    return sums


def start_rows(mixed, aux_ref):
    total = mixed[:, 3:4] * aux_ref[3:4, :]
    for j in range(3):
        total = total + mixed[:, j : j + 1] * aux_ref[j : j + 1, :]
    return total


def first_kernel(
    place_ref, mixed_ref, aux_ref, cond_own, cond_other, rows_own, rows_other, out_own, out_other, w0, w1, w2, w3,
    before_ref, gated_ref, next_ref, start_ref, out_ref, taps_ref, sem,
):
    step = pl.program_id(0)
    sources = (w0, w1, w2, w3)
    per_crop = pl.num_programs(0) // mixed_ref.shape[0]
    margin = FIRST_DILATION

    @pl.when(step == 0)
    def _():
        fetch_taps(place_ref, sources, taps_ref, sem, 0)
        for crop in range(mixed_ref.shape[0]):
            start_ref[crop] = start_rows(mixed_ref[crop], aux_ref).astype(jnp.bfloat16)
        for core, piece in enumerate((out_own, out_other)):
            for across in range(2):
                column = pl.multiple_of(place_ref[NMAT + 8 + 2 * core + across] * 128, 128)
                for t in range(8):
                    spot = place_ref[NMAT + t]
                    for matrix in range(3):
                        out_ref[matrix, 64 * t : 64 * t + 64, pl.ds(column, 128)] = piece[
                            spot, across, matrix
                        ]
        await_taps(sources, taps_ref, sem)

    crop = step // per_crop
    base = pl.multiple_of((step % per_crop) * ROWS, ROWS)
    left, right = gate_inputs(
        0, place_ref, (cond_own, cond_other), (rows_own, rows_other), aux_ref, start_ref, crop, base, margin, taps_ref
    )
    before_ref[:, :H] = left
    before_ref[:, H:] = right
    gated = (jnp.tanh(left) * sigmoid(right)).astype(jnp.bfloat16)
    gated_ref[...] = gated
    hidden = start_rows(mixed_ref[crop, pl.ds(base + margin, ROWS), :], aux_ref)
    hidden = hidden + dot_as(NN, gated, out_ref[0]) + aux_ref[8:9, :]
    next_ref[...] = hidden.astype(jnp.bfloat16)


def second_kernel(
    place_ref, scale_ref, flow_ref, own_ref, before_halo, after_halo, aux_ref, cells_ref,
    cond_own, cond_other, rows_own, rows_other, gated_ref, out_ref, w0, w1, w2, w3,
    skip_ref, grads_ref, low_ref, mixed_ref, sums_ref, taps_ref, wide_ref, end_ref, sem,
):
    step = pl.program_id(0)
    sources = (w0, w1, w2, w3)
    crops, length = own_ref.shape[:2]
    margin = 2 * FIRST_DILATION

    @pl.when(step == 0)
    def _():
        fetch_taps(place_ref, sources, taps_ref, sem, 1)
        wide_ref[:, :margin] = before_halo[...]
        wide_ref[:, margin : margin + length] = own_ref[...]
        wide_ref[:, margin + length :] = after_halo[...]
        sums_ref[...] = jnp.zeros_like(sums_ref)
        end_ref[...] = jnp.zeros_like(end_ref)
        end_ref[0:6] = aux_ref[11:17, :]
        await_taps(sources, taps_ref, sem)

    per_crop = length // ROWS
    crop = step // per_crop
    base = pl.multiple_of((step % per_crop) * ROWS, ROWS)
    left, right = gate_inputs(
        1, place_ref, (cond_own, cond_other), (rows_own, rows_other), aux_ref, wide_ref, crop, base, margin, taps_ref
    )
    tangent, part = jnp.tanh(left), sigmoid(right)
    gated = (tangent * part).astype(jnp.bfloat16)
    skip_ref[...] = gated
    total = dot_as(NN, gated_ref[...], out_ref[1]) + dot_as(NN, gated, out_ref[2])
    total = total + (aux_ref[9:10, :] + aux_ref[10:11, :])
    halves_total = _split(total)
    outputs = _three(DNT, halves_total, _split(end_ref[...]))
    lane = lax.broadcasted_iota(jnp.int32, outputs.shape, 1)
    row_lane = lane[0:1]
    bias = jnp.zeros((1, 128), jnp.float32)
    for j in range(6):
        bias = jnp.where(row_lane == j, flow_ref[j, 6], bias)
    outputs = outputs + bias
    inside = lane < 3
    log_scale = jnp.where(inside, outputs, 0.0)
    growth = jnp.exp(log_scale)
    cells = cells_ref[crop, pl.ds(base + FIRST_DILATION, ROWS), :]
    upper = jnp.concatenate([cells, jnp.zeros((ROWS, 120), jnp.float32)], axis=1)
    upper = jnp.where(inside, pltpu.roll(upper, 124, axis=1), 0.0)
    z_upper = jnp.where(inside, growth * upper + pltpu.roll(outputs, 125, axis=1), 0.0)
    scale = scale_ref[0]
    grad_z = scale * z_upper
    grad_upper = grad_z * growth
    mixed_ref[...] = grad_upper[:, :8]
    grad_log = jnp.where(inside, grad_upper * upper - scale, 0.0)
    grad_outputs = grad_log + pltpu.roll(grad_z, 3, axis=1)
    grad_skip = grad_outputs[:, 0:1] * end_ref[0:1, :]
    for j in range(1, 6):
        grad_skip = grad_skip + grad_outputs[:, j : j + 1] * end_ref[j : j + 1, :]
    grad_skip = grad_skip.astype(jnp.bfloat16)
    grads_ref[...] = grad_skip
    grad_gated = dot_as(DNT, grad_skip, out_ref[2])
    grad_left = (grad_gated * (1.0 - tangent * tangent) * part).astype(jnp.bfloat16)
    grad_right = (grad_gated * tangent * part * (1.0 - part)).astype(jnp.bfloat16)
    low_ref[:, :H] = grad_left
    low_ref[:, H:] = grad_right
    sums_ref[0:8] += _three(DTN, _split(grad_outputs), halves_total)[0:8]
    sums_ref[8:9] += jnp.sum(grad_left.astype(jnp.float32), axis=0, keepdims=True)
    sums_ref[9:10] += jnp.sum(grad_right.astype(jnp.float32), axis=0, keepdims=True)
    sums_ref[10:11] += jnp.sum(grad_skip.astype(jnp.float32), axis=0, keepdims=True)
    sums_ref[11:12, :128] += jnp.sum(grad_outputs, axis=0, keepdims=True)
    sums_ref[12:13, :128] += jnp.sum(0.5 * z_upper * z_upper - log_scale, axis=0, keepdims=True)


def third_kernel(
    place_ref, own_ref, before_halo, after_halo, grads_ref, before_ref, out_ref, w0, w1, w2, w3,
    hidden_ref, residual_ref, low_ref, sums_ref, taps_ref, wide_ref, sem,
):
    step = pl.program_id(0)
    sources = (w0, w1, w2, w3)
    crops, length = own_ref.shape[:2]
    margin = 2 * FIRST_DILATION

    @pl.when(step == 0)
    def _():
        fetch_taps(place_ref, sources, taps_ref, sem, 1)
        wide_ref[:, :margin] = before_halo[...]
        wide_ref[:, margin : margin + length] = own_ref[...]
        wide_ref[:, margin + length :] = after_halo[...]
        sums_ref[...] = jnp.zeros_like(sums_ref)
        await_taps(sources, taps_ref, sem)

    per_crop = length // ROWS
    crop = step // per_crop
    base = pl.multiple_of((step % per_crop) * ROWS, ROWS)
    total = None
    for k in range(3):
        for half in range(2):
            window = wide_ref[crop, pl.ds(base + margin * (2 - k), ROWS), H * half : H * half + H]
            part = dot_as(DNT, window, taps_ref[2 * k + half])
            total = part if total is None else total + part
    hidden_ref[...] = total
    residual = total.astype(jnp.bfloat16)
    residual_ref[...] = residual
    grad_gated = dot_as(DNT, grads_ref[...], out_ref[1]) + dot_as(DNT, residual, out_ref[0])
    tangent, part = jnp.tanh(before_ref[:, :H]), sigmoid(before_ref[:, H:])
    grad_left = (grad_gated * (1.0 - tangent * tangent) * part).astype(jnp.bfloat16)
    grad_right = (grad_gated * tangent * part * (1.0 - part)).astype(jnp.bfloat16)
    low_ref[:, :H] = grad_left
    low_ref[:, H:] = grad_right
    sums_ref[0:1] += jnp.sum(residual.astype(jnp.float32), axis=0, keepdims=True)
    sums_ref[1:2] += jnp.sum(grad_left.astype(jnp.float32), axis=0, keepdims=True)
    sums_ref[2:3] += jnp.sum(grad_right.astype(jnp.float32), axis=0, keepdims=True)


def taps_kernel(place_ref, *refs, layer, pieces, owned):
    inputs, low_ref = refs[:pieces], refs[pieces]
    outs = refs[-3 - 2 * owned : -3]
    wide_ref, buffer_ref, sem = refs[-3:]
    crops, length = low_ref.shape[:2]
    margin = FIRST_DILATION * 2**layer
    offset = 0
    for piece in inputs:
        width = piece.shape[1]
        for crop in range(crops):
            wide_ref[crop, offset : offset + width] = piece[crop]
        offset += width
    for k in range(3):
        for half in range(2):
            j = 2 * k + half
            total = None
            for crop in range(crops):
                window = wide_ref[crop, margin * k : margin * k + length]
                part = dot_as(DTN, window, low_ref[crop, :, H * half : H * half + H])
                total = part if total is None else total + part
            buffer_ref[j] = total.astype(jnp.bfloat16)
            place = place_ref[6 * layer + j]
            relation = place // owned
            target = (relation // 2) * owned + place % owned
            for d, out_ref in enumerate(outs):

                @pl.when(target == d)
                def _(out_ref=out_ref):
                    pltpu.make_async_copy(buffer_ref.at[j], out_ref.at[relation % 2], sem.at[j]).start()

    for j in range(6):
        pltpu.make_async_copy(buffer_ref.at[j], outs[0].at[0], sem.at[j]).wait()


def start_kernel(
    place_ref, low_ref, above_ref, cells_ref, aux_ref, w0, w1, w2, w3,
    start_ref, lower_ref, taps_ref, wide_ref, end_ref, sem,
):
    crop = pl.program_id(0)
    sources = (w0, w1, w2, w3)
    length = low_ref.shape[1]
    margin = FIRST_DILATION

    @pl.when(crop == 0)
    def _():
        fetch_taps(place_ref, sources, taps_ref, sem, 0)
        start_ref[...] = jnp.zeros_like(start_ref)
        end_ref[...] = jnp.zeros_like(end_ref)
        end_ref[0:3] = aux_ref[0:3, :]
        await_taps(sources, taps_ref, sem)

    wide_ref[...] = jnp.zeros_like(wide_ref)
    wide_ref[margin : margin + length] = above_ref[...]
    for k in range(3):
        flowing = dot_as(DNT, low_ref[0, :, :H], taps_ref[2 * k])
        flowing = flowing + dot_as(DNT, low_ref[0, :, H:], taps_ref[2 * k + 1])
        wide_ref[margin * k : margin * k + length] += flowing
    pieces = _split(wide_ref[...])
    cells = cells_ref[crop]
    cells = jnp.concatenate([cells, jnp.zeros((cells.shape[0], 120), jnp.float32)], axis=1)
    start_ref[...] += _three(DTN, _split(cells), pieces)[0:8]
    lower_ref[0] = _three(DNT, pieces, _split(end_ref[...]))[:, :8]


def smem():
    return pl.BlockSpec(memory_space=pltpu.SMEM)


def vmem():
    return pl.BlockSpec(memory_space=pltpu.VMEM)


def anywhere():
    return pl.BlockSpec(memory_space=pl.ANY)


def by_rows(width):
    return pl.BlockSpec((ROWS, width), lambda i: (i, 0))


def fixed(shape, index):
    return pl.BlockSpec(shape, lambda i: index)


def shaped(shape, dtype=jnp.float32):
    return jax.ShapeDtypeStruct(shape, dtype)


def taps_gradient(place, pieces, low, layer, owned, targets=()):
    crops, length = low.shape[:2]
    width = sum(piece.shape[1] for piece in pieces)
    return pl.pallas_call(
        lambda *refs: taps_kernel(*refs, layer=layer, pieces=len(pieces), owned=owned),
        out_shape=[shaped((2, H, H), jnp.bfloat16)] * (2 * owned),
        in_specs=[smem()] + [vmem() for _ in pieces] + [vmem()] + [anywhere() for _ in targets],
        out_specs=[anywhere()] * (2 * owned),
        scratch_shapes=[
            pltpu.VMEM((crops, width, H), jnp.bfloat16),
            pltpu.VMEM((6, H, H), jnp.bfloat16),
            pltpu.SemaphoreType.DMA((6,)),
        ],
        input_output_aliases={len(pieces) + 2 + i: i for i in range(len(targets))},
        name=f"taps_gradient_{layer}",
    )(place, *pieces, low, *targets)


def halo(cells, width):
    count = lax.axis_size("tm")
    head, tail = cells[:, :width], cells[:, cells.shape[1] - width :]
    return (
        lax.ppermute(tail, "tm", [(i, i + 1) for i in range(count - 1)]),
        lax.ppermute(head, "tm", [(i + 1, i) for i in range(count - 1)]),
    )


def gather_relative(values, axis, bits):
    for bit in bits:
        values = jnp.concatenate([values, swap(values, axis, bit)], axis=0)
    return values


def reduced_slot(kept, sent):
    other = yield sent, "opt", 1
    sent, kept = kept[1] + other[1], kept[0] + other[0]
    other = yield sent, "opt", 2
    part = kept.astype(jnp.float32) + other.astype(jnp.float32)
    bits = bits_of("tm")
    for bit in bits[:-1]:
        kept, sent = halves(part, "tm", bit, 0)
        other = yield sent.astype(jnp.bfloat16), "tm", bit
        part = kept + other.astype(jnp.float32)
    part = part.astype(jnp.bfloat16)
    other = yield part, "tm", bits[-1]
    part = part + other
    for bit in reversed(bits[:-1]):
        other = yield part, "tm", bit
        part = ordered(part, other, "tm", bit, 0)
    return part


def swap_all(values, axis, bit):
    return jax.tree.map(lambda value: swap(value, axis, bit), values)


def lowest_half(values, bit, dim):
    shape = values.shape
    values = values.reshape(*shape[:dim], shape[dim] // 2, 2, *shape[dim + 1 :])
    kept, sent = halves(values, "tm", bit, dim + 1)
    shape = (*shape[:dim], shape[dim] // 2, *shape[dim + 1 :])
    return kept.reshape(shape), sent.reshape(shape)


def wide(values):
    return jax.tree.map(lambda value: value.astype(jnp.float32), values)


def narrow(values):
    return jax.tree.map(lambda value: value.astype(jnp.bfloat16), values)


def spread_rest(cond, out, small):
    other = yield (cond[1], out[1], small), "opt", 1
    cond = [mine + theirs for mine, theirs in zip(cond[0], wide(other[0]))]
    out, small = out[0] + wide(other[1]), small + other[2]
    width = cond[0].shape[0] // 2
    other = yield (narrow([part[width:] for part in cond]), narrow(out[1]), small), "opt", 2
    cond = [mine[:width] + theirs for mine, theirs in zip(cond, wide(other[0]))]
    out, small = out[0] + wide(other[1]), small + other[2]
    count = lax.axis_size("tm")
    cond = jnp.concatenate(cond, axis=1).reshape(width, count, -1)
    cond = jnp.swapaxes(cond, 0, 1)
    out = out.reshape(out.shape[0], count, -1, out.shape[2])
    for bit in bits_of("tm"):
        cond, sent = lowest_half(cond, bit, 0)
        out, sent_out = lowest_half(out, bit, 1)
        other = yield (narrow(sent), narrow(sent_out), small), "tm", bit
        cond, out, small = cond + wide(other[0]), out + wide(other[1]), small + other[2]
    return cond[0].T, out[:, 0], small


def reduce_slots(keep, send, work, follow, entry):
    owned = len(keep)
    chunks = [reduced_slot(kept, sent) for kept, sent in zip(keep, send)]
    requests = {i: next(chunk) for i, chunk in enumerate(chunks)}
    answers, ready, stage = {}, {}, {}
    done, results, latest, held = {}, [], (), None
    slot = 0
    while len(done) < owned:
        for i in [i for i in answers if ready[i] == slot]:
            try:
                requests[i] = chunks[i].send(answers.pop(i))
            except StopIteration as stop:
                done[i] = stop.value
                continue
            if i == owned and requests[i][1] == "tm":
                held = requests.pop(i)
        if slot == entry:
            chunks.append(follow(results + [latest]))
            requests[owned] = next(chunks[owned])
        active = sorted(requests)
        task, inputs = work.get(slot, (None, ()))
        values, inputs, latest = lax.optimization_barrier(
            (tuple(requests[i][0] for i in active), inputs, latest)
        )
        if slot - 1 in work:
            results.append(latest)
        for value, i in zip(values, active):
            answers[i] = swap_all(value, *requests[i][1:])
            stage[i] = stage.get(i, 0) + 1
            ready[i] = slot + 1
            if i < owned and stage[i] == 1:
                ready[i] = 1 if i == 0 else 2
            if i < owned and stage[i] == 2:
                ready[i] = 3 + i
        latest = () if task is None else task(*inputs)
        requests = {}
        slot += 1
    total = jnp.stack([done[i] for i in range(owned)])
    value, total = lax.optimization_barrier((held[0], total))
    return total, [chunks[owned], value, held[1:]]


def advance(rest, tied):
    chunk, value, where = rest
    answer, tied = lax.optimization_barrier((swap_all(value, *where), tied))
    try:
        rest[1], *rest[2:] = (lambda value, *where: (value, where))(*chunk.send(answer))
    except StopIteration as stop:
        rest[:] = [None, stop.value, None]
    return tied


def finish(rest):
    while rest[0] is not None:
        try:
            value, *where = rest[0].send(swap_all(rest[1], *rest[2]))
            rest[1:] = [value, where]
        except StopIteration as stop:
            rest[:] = [None, stop.value, None]
    return rest[1]


def adamw_update(weight, gradient, moment_one, moment_two, steps_done, rate_value):
    moment_one = beta_first * moment_one + (1.0 - beta_first) * gradient
    moment_two = beta_second * moment_two + (1.0 - beta_second) * gradient * gradient
    direction = (
        moment_one
        / (1.0 - beta_first**steps_done)
        / (jnp.sqrt(moment_two / (1.0 - beta_second**steps_done)) + epsilon)
    )
    weight = weight - rate_value * (direction + decay_weight * weight)
    return (weight, moment_one, moment_two)


def shards(
    wave,
    crop_offsets,
    squeeze_order,
    mel,
    mel_index,
    soap_slots,
    step_count,
    in_weight,
    soap_first,
    soap_second,
    left_stats,
    right_stats,
    left_basis,
    right_basis,
    cond_weight,
    cond_first,
    cond_second,
    out_weight,
    out_first,
    out_second,
    aux_params,
    aux_first,
    aux_second,
    flow_params,
    flow_first,
    flow_second,
):
    crops_current = wave.shape[0]
    row_count = crops_current * G_DEV
    tokens_all = row_count * lax.axis_size("tm") * lax.axis_size("opt")
    scale_final = 1.0 / (6.0 * tokens_all)
    scale_early = early_weight / (2.0 * tokens_all)
    steps_done = step_count[0].astype(jnp.float32)
    owned = in_weight.shape[0]
    rank = lax.axis_index("opt")
    own = in_weight.astype(jnp.bfloat16)
    cond_part = cond_weight.astype(jnp.bfloat16).T
    out_part = out_weight.astype(jnp.bfloat16)[None]
    own, cond_part, out_part = lax.optimization_barrier((own, cond_part, out_part))
    cond_across, out_across = swap(cond_part, "opt", 2), swap(out_part, "opt", 2)
    own, cond_part, cond_across, out_part, out_across, wave, mel_index = lax.optimization_barrier(
        (own, cond_part, cond_across, out_part, out_across, wave, mel_index)
    )
    tm_rank, tm_bits = lax.axis_index("tm"), bits_of("tm")[::-1]
    count_tm = lax.axis_size("tm")
    segments = [
        lax.dynamic_slice_in_dim(wave[crop, 0], crop_offsets[crop], 8 * G_DEV, 0).reshape(G_DEV, 8)
        for crop in range(crops_current)
    ]
    chosen = jnp.arange(8, dtype=jnp.int32)[:, None] == squeeze_order[None, :]
    squeezed = full_dot(jnp.concatenate(segments), chosen.astype(jnp.float32))
    squeezed = squeezed.reshape(crops_current, G_DEV, 8)
    flow_matrix = flow_params[:, :6]
    mixed = full_dot(squeezed.reshape(row_count, 8)[:, 2:], flow_matrix.T)
    lower_half, upper_half = mixed[:, :3], mixed[:, 3:]
    cells = jnp.concatenate(
        [
            lower_half,
            jnp.ones((row_count, 1), jnp.float32),
            upper_half,
            jnp.zeros((row_count, 1), jnp.float32),
        ],
        axis=1,
    ).reshape(crops_current, G_DEV, 8)
    edge = jnp.concatenate([cells, squeezed], axis=2)
    edge_before, edge_after = halo(edge, FIRST_DILATION)
    edge = jnp.concatenate([edge_before, edge, edge_after], axis=1)
    cells_wide, squeezed_wide = edge[..., :8], edge[..., 8:]

    slots = jnp.arange(NMAT, dtype=jnp.int32)
    slot_of = jnp.sum(
        jnp.where(soap_slots[None, :] == slots[:, None], slots[None, :], 0), axis=1
    ).astype(jnp.int32)
    relation = (slot_of // owned) ^ rank
    place = ((relation % 2) * 2 + relation // 2) * owned + slot_of % owned

    spots = jnp.zeros((count_tm,), jnp.int32)
    for index, bit in enumerate(tm_bits):
        distance = jnp.arange(count_tm, dtype=jnp.int32) ^ tm_rank
        spots = spots + ((distance // bit) % 2) * (1 << index)
    columns = rank ^ jnp.array([0, 2, 1, 3], jnp.int32)

    across = swap(own, "opt", 2)
    cond_part = jnp.concatenate([cond_part, cond_across], axis=0)[None]
    out_part = jnp.concatenate([out_part, out_across], axis=0)[None]
    own_core = swap(own, "opt", 1)
    across_core = swap(across, "opt", 1)
    sources = (own, across, own_core, across_core)
    cond_part = gather_relative(cond_part, "tm", tm_bits)
    out_part = gather_relative(out_part, "tm", tm_bits)
    if count_tm != 8:
        fold = count_tm // 8
        cond_part = jnp.take(cond_part, spots, axis=0)
        cond_part = cond_part.reshape(8, fold, *cond_part.shape[1:])
        cond_part = jnp.moveaxis(cond_part, 1, 2).reshape(8, cond_part.shape[2], -1)
        out_part = jnp.take(out_part, spots, axis=0)
        out_part = out_part.reshape(8, fold, *out_part.shape[1:])
        out_part = jnp.moveaxis(out_part, 1, 3).reshape(8, 2, 3, 64, -1)
        spots = jnp.arange(8, dtype=jnp.int32)
    place = jnp.concatenate([place, spots, columns])

    spot_of = jnp.arange(2 * 4 * FR_DEV, dtype=jnp.int32)
    quarter = (spot_of // FR_DEV) % 4
    sample = 2 * (rank ^ (spot_of // (4 * FR_DEV)) ^ (2 * (quarter // 2))) + quarter % 2
    spread = (jnp.arange(8, dtype=jnp.int32)[:, None] == sample[None, :]).astype(jnp.bfloat16)
    frames = half_dot(mel_index.reshape(row_count, 8).astype(jnp.bfloat16), spread)
    hits = (frames == (spot_of % FR_DEV).astype(jnp.float32)[None, :]).astype(jnp.bfloat16)
    hits = hits.reshape(crops_current, G_DEV, 2, 4 * FR_DEV)
    same = jnp.eye(4, dtype=jnp.bfloat16)
    frame_blocks = (same[None, :, None, :, None] * mel[:, None, :, None, :]).reshape(
        crops_current, 4 * FR_DEV, 4 * MEL
    )
    cond_rows = tuple(
        jnp.einsum(
            "cgk,ckm->cgm", hits[:, :, side], frame_blocks, preferred_element_type=jnp.float32
        )
        .astype(jnp.bfloat16)
        .reshape(row_count, 4 * MEL)
        for side in (0, 1)
    )
    cond_part, out_part, cond_rows, cells_wide, squeezed_wide, place = lax.optimization_barrier(
        (cond_part, out_part, cond_rows, cells_wide, squeezed_wide, place)
    )
    cond_other = swap(cond_part, "opt", 1)
    out_other = swap(out_part, "opt", 1)
    steps = row_count // ROWS
    taps_scratch = [pltpu.VMEM((6, H, H), jnp.bfloat16)]
    sems = [pltpu.SemaphoreType.DMA((6,))]
    half_cols = 4 * MEL
    wide_rows = G_DEV + 2 * FIRST_DILATION
    before_first, gated_first, hidden_low, start_low, out_full = pl.pallas_call(
        first_kernel,
        grid=(steps,),
        out_shape=[
            shaped((row_count, 2 * H)),
            shaped((row_count, H), jnp.bfloat16),
            shaped((row_count, H), jnp.bfloat16),
            shaped((crops_current, wide_rows, H), jnp.bfloat16),
            shaped((3, H, H), jnp.bfloat16),
        ],
        in_specs=[smem(), vmem(), vmem(), by_rows(half_cols), by_rows(half_cols)]
        + [vmem()] * 4
        + [anywhere()] * 4,
        out_specs=[by_rows(2 * H), by_rows(H), by_rows(H), vmem(), vmem()],
        scratch_shapes=taps_scratch + sems,
        name="first_layer",
    )(
        place,
        cells_wide,
        aux_params,
        *cond_rows,
        cond_part,
        cond_other,
        out_part,
        out_other,
        *sources,
    )

    hidden_low = hidden_low.reshape(crops_current, G_DEV, H)
    margin = 2 * FIRST_DILATION
    hidden_halo = halo(hidden_low, margin)
    gated_second, grad_skip, low_second, grad_upper, sums_second = pl.pallas_call(
        second_kernel,
        grid=(steps,),
        out_shape=[
            shaped((row_count, H), jnp.bfloat16),
            shaped((row_count, H), jnp.bfloat16),
            shaped((row_count, 2 * H), jnp.bfloat16),
            shaped((row_count, 8)),
            shaped((16, H)),
        ],
        in_specs=[smem(), smem(), smem(), vmem(), vmem(), vmem(), vmem(), vmem()]
        + [by_rows(half_cols)] * 2
        + [vmem()] * 2
        + [by_rows(H), vmem()]
        + [anywhere()] * 4,
        out_specs=[by_rows(H), by_rows(H), by_rows(2 * H), by_rows(8), vmem()],
        scratch_shapes=taps_scratch
        + [pltpu.VMEM((crops_current, G_DEV + 2 * margin, H), jnp.bfloat16)]
        + [pltpu.VMEM((128, H), jnp.float32)]
        + sems,
        name="second_layer",
    )(
        place,
        jnp.full((1,), scale_final, jnp.float32),
        flow_params,
        hidden_low,
        *hidden_halo,
        aux_params,
        cells_wide,
        *cond_rows,
        cond_part,
        cond_other,
        gated_first,
        out_full,
        *sources,
    )
    low_cells = low_second.reshape(crops_current, G_DEV, 2 * H)
    low_halo = halo(low_cells, margin)
    grad_slots = taps_gradient(
        place, (hidden_halo[0], hidden_low, hidden_halo[1]), low_cells, 1, owned
    )
    grad_hidden, grad_residual, low_first, sums_first = pl.pallas_call(
        third_kernel,
        grid=(steps,),
        out_shape=[
            shaped((row_count, H)),
            shaped((row_count, H), jnp.bfloat16),
            shaped((row_count, 2 * H), jnp.bfloat16),
            shaped((8, H)),
        ],
        in_specs=[smem(), vmem(), vmem(), vmem(), by_rows(H), by_rows(2 * H), vmem()]
        + [anywhere()] * 4,
        out_specs=[by_rows(H), by_rows(H), by_rows(2 * H), vmem()],
        scratch_shapes=taps_scratch
        + [pltpu.VMEM((crops_current, G_DEV + 2 * margin, 2 * H), jnp.bfloat16)]
        + sems,
        name="first_gradient",
    )(place, low_cells, *low_halo, grad_skip, before_first, out_full, *sources)
    low_first_cells = low_first.reshape(crops_current, G_DEV, 2 * H)
    grad_slots = taps_gradient(place, (start_low,), low_first_cells, 0, owned, grad_slots)
    def start_work(low, above, cells):
        start, lower = pl.pallas_call(
            start_kernel,
            grid=(crops_current,),
            out_shape=[shaped((8, H)), shaped((crops_current, wide_rows, 8))],
            in_specs=[
                smem(),
                pl.BlockSpec((1, G_DEV, 2 * H), lambda i: (i, 0, 0)),
                pl.BlockSpec((G_DEV, H), lambda i: (i, 0)),
                vmem(),
                vmem(),
            ]
            + [anywhere()] * 4,
            out_specs=[vmem(), pl.BlockSpec((1, wide_rows, 8), lambda i: (i, 0, 0))],
            scratch_shapes=taps_scratch
            + [pltpu.VMEM((wide_rows, H), jnp.float32), pltpu.VMEM((128, H), jnp.float32)]
            + sems,
            name="start_gradient",
        )(place, low, above, cells, aux_params, *sources)
        return (start[:4], lower.reshape(-1, 8)[:, :3])

    def cond_work(own_rows, other_rows, first, second):
        return tuple(
            tuple(rows_dot(rows, low).astype(kind) for low in (first, second))
            for rows, kind in ((own_rows, jnp.float32), (other_rows, jnp.bfloat16))
        )

    def out_work(first, second, above, skip):
        pairs = ((first, above), (first, skip), (second, skip))
        grads = jnp.stack([rows_dot(*pair) for pair in pairs])
        return tuple(
            jnp.stack(
                [
                    lax.dynamic_slice_in_dim(grads, (rank ^ core ^ bit) * 128, 128, 2)
                    for bit in (0, 2)
                ]
            )
            for core in (0, 1)
        )

    def out_parts(*inputs):
        own, other = out_work(*inputs)
        return own, other.astype(jnp.bfloat16)

    def rest_of(results):
        (grad_start, grad_lower), grad_cond, grad_out = results
        final_part = jnp.sum(sums_second[12]) + 0.5 * jnp.sum(lower_half * lower_half)
        early_part = 0.5 * jnp.sum(squeezed[..., :2] * squeezed[..., :2])
        flow_lower = rows_dot(grad_lower, squeezed_wide.reshape(-1, 8)[:, 2:], highest)
        flow_lower = flow_lower + scale_final * rows_dot(
            lower_half, squeezed.reshape(-1, 8)[:, 2:], highest
        )
        flow_upper = rows_dot(grad_upper[:, :3], squeezed.reshape(-1, 8)[:, 2:], highest)
        grad_flow = jnp.concatenate(
            [jnp.concatenate([flow_lower, flow_upper], axis=0), sums_second[11, :6][:, None]], axis=1
        )
        grad_aux = jnp.concatenate(
            [
                grad_start,
                sums_first[1:3],
                sums_second[8:10],
                sums_first[0:1],
                sums_second[10:11],
                sums_second[10:11],
                sums_second[0:6],
            ],
            axis=0,
        )
        small = jnp.concatenate(
            [grad_aux.reshape(-1), grad_flow.reshape(-1), jnp.stack([final_part, early_part])]
        )
        small = jnp.pad(small, (0, -small.shape[0] % 1024)).reshape(-1, 128)
        return spread_rest(grad_cond, grad_out, small)

    grad_owned, rest = reduce_slots(
        grad_slots[:owned],
        grad_slots[owned:],
        {
            2: (start_work, (low_first_cells, grad_hidden, cells_wide)),
            3: (cond_work, (*cond_rows, low_first, low_second)),
            4: (out_parts, (gated_first, gated_second, grad_residual, grad_skip)),
        },
        rest_of,
        5,
    )
    grad_owned = grad_owned.astype(jnp.float32)
    (
        in_new,
        soap_first_new,
        soap_second_new,
        left_stats_new,
        right_stats_new,
        left_basis_new,
        right_basis_new,
    ) = soap_update(
        in_weight,
        grad_owned,
        soap_first,
        soap_second,
        left_stats,
        right_stats,
        left_basis,
        right_basis,
        steps_done,
        rest,
    )
    grad_cond, grad_out, small = finish(rest)
    small = small.reshape(-1)
    filled = aux_params.size + flow_params.size + 2
    grad_aux = small[: aux_params.size].reshape(aux_params.shape)
    grad_flow = small[aux_params.size : filled - 2].reshape(flow_params.shape)
    parts = small[filled - 2 : filled]
    factor = jnp.linalg.cholesky(full_dot(flow_matrix, flow_matrix.T))
    log_det = jnp.sum(jnp.log(jnp.diagonal(factor)))
    inverse_t = jax.scipy.linalg.cho_solve((factor, True), flow_matrix)
    grad_flow = grad_flow.at[:, :6].add(-inverse_t / 6.0)
    loss = parts[0] * scale_final + parts[1] * scale_early - log_det / 6.0
    cond_new, cond_first_new, cond_second_new = adamw_update(
        cond_weight, grad_cond, cond_first, cond_second, steps_done, learn_rate
    )
    out_new, out_first_new, out_second_new = adamw_update(
        out_weight, grad_out, out_first, out_second, steps_done, learn_rate
    )
    aux_new, aux_first_new, aux_second_new = adamw_update(
        aux_params, grad_aux, aux_first, aux_second, steps_done, aux_rate
    )
    flow_new, flow_first_new, flow_second_new = adamw_update(
        flow_params, grad_flow, flow_first, flow_second, steps_done, learn_rate
    )
    return (
        loss,
        in_new,
        soap_first_new,
        soap_second_new,
        left_stats_new,
        right_stats_new,
        left_basis_new,
        right_basis_new,
        cond_new,
        cond_first_new,
        cond_second_new,
        out_new,
        out_first_new,
        out_second_new,
        aux_new,
        aux_first_new,
        aux_second_new,
        flow_new,
        flow_first_new,
        flow_second_new,
    )


def solution(mesh):
    placed = (
        P("opt", "tm", None),
        P("opt"),
        P(),
        P("opt", "tm", None),
        P("opt", "tm", None),
        P(),
        P(),
        P("opt", None, None),
        P("opt", None, None),
        P("opt", None, None),
        P("opt", None, None),
        P("opt", None, None),
        P("opt", None, None),
        P("opt", None, None),
        P("tm", "opt"),
        P("tm", "opt"),
        P("tm", "opt"),
        P(None, "tm", "opt"),
        P(None, "tm", "opt"),
        P(None, "tm", "opt"),
        P(),
        P(),
        P(),
        P(),
        P(),
        P(),
    )
    return jax.shard_map(
        shards,
        mesh=mesh,
        in_specs=placed,
        out_specs=(
            P(),
            P("opt", None, None),
            P("opt", None, None),
            P("opt", None, None),
            P("opt", None, None),
            P("opt", None, None),
            P("opt", None, None),
            P("opt", None, None),
            P("tm", "opt"),
            P("tm", "opt"),
            P("tm", "opt"),
            P(None, "tm", "opt"),
            P(None, "tm", "opt"),
            P(None, "tm", "opt"),
            P(),
            P(),
            P(),
            P(),
            P(),
            P(),
        ),
        check_vma=False,
    )
```

```python
import jax
import jax.numpy as jnp
from jax import lax
from jax.experimental import pallas as pl
from jax.experimental.pallas import tpu as pltpu
from jax.sharding import PartitionSpec as P

H = 512
MEL = 80
LAYERS = 2
FIRST_DILATION = 64
G_DEV = 512
FR_DEV = 16
NMAT = 12


highest = lax.Precision.HIGHEST
beta_first = 0.9
beta_second = 0.99
beta_stats = 0.95
learn_rate = 0.02
aux_rate = 0.15
epsilon = 1e-08
decay_weight = 0.01
early_weight = 0.5


def full_dot(matrix_a, matrix_b):
    return jnp.dot(matrix_a, matrix_b, precision=highest, preferred_element_type=jnp.float32)


def half_dot(matrix_a, matrix_b):
    return jnp.dot(matrix_a, matrix_b, preferred_element_type=jnp.float32)


def rows_dot(matrix_a, matrix_b, exactness=None):
    return lax.dot_general(
        matrix_a,
        matrix_b,
        (((0,), (0,)), ((), ())),
        precision=exactness,
        preferred_element_type=jnp.float32,
    )


def cols_dot(matrix_a, matrix_b):
    return lax.dot_general(
        matrix_a, matrix_b, (((1,), (1,)), ((), ())), preferred_element_type=jnp.float32
    )


PIVOTS = 8


def _nt(x, y):
    return _three(NT, _split(x), _split(y))


def _nn(x, y):
    return _three(NN, _split(x), _split(y))


def _split(x):
    hi = x.astype(jnp.bfloat16)
    return hi, (x - hi.astype(jnp.float32)).astype(jnp.bfloat16)

def _three(dims, x, y):
    xh, xl = x
    yh, yl = y
    dot = lambda a, b: lax.dot_general(a, b, dims, preferred_element_type=jnp.float32)
    return dot(xh, yh) + (dot(xh, yl) + dot(xl, yh))

NT = (((1,), (1,)), ((), ()))
NN = (((1,), (0,)), ((), ()))

def pair_inverse(blocks):
    lane = lax.broadcasted_iota(jnp.int32, (8, 128), 1)
    sub = lax.broadcasted_iota(jnp.int32, (8, 128), 0)
    local = lane % 64
    half = lane - local
    groups = [[block[8 * g:8 * g + 8] for g in range(8)] for block in blocks]
    for start in range(0, 64, PIVOTS):
        first, low = divmod(start, 8)
        inside = (local >= start) & (local < start + PIVOTS)
        for rows in groups:
            cols = []
            for n in range(PIVOTS):
                pick = half + (start + n)
                cols.append([jnp.take_along_axis(rows[g], pick, axis=1, mode="promise_in_bounds") for g in range(first, 8)])
            lead = rows[first]
            entry = [[cols[n][0][low + m:low + m + 1] for n in range(m + 1)] for m in range(PIVOTS)]
            work = [jnp.where(local == start + m, 1.0, jnp.where(inside, 0.0, jnp.broadcast_to(lead[low + m:low + m + 1], (8, 128)))) for m in range(PIVOTS)]
            entry = [[jnp.broadcast_to(e, (8, 128)) for e in line] for line in entry]
            scaled = []
            ratio = {}
            for m in range(PIVOTS):
                inverse = 1.0 / entry[m][m]
                for n in range(m + 1, PIVOTS):
                    ratio[n, m] = entry[n][m] * inverse
                for n in range(m + 1, PIVOTS):
                    work[n] = work[n] - ratio[n, m] * work[m]
                    for q in range(m + 1, n + 1):
                        entry[n][q] = entry[n][q] - ratio[n, m] * entry[q][m]
                scaled.append(work[m] * inverse)
            final = [work[m] * lax.rsqrt(entry[m][m]) for m in range(PIVOTS)]
            for m in range(PIVOTS - 2, -1, -1):
                for n in range(m + 1, PIVOTS):
                    scaled[m] = scaled[m] - ratio[n, m] * scaled[n]
            for g in range(first, 8):
                old = jnp.where(inside, 0.0, rows[g])
                new = old
                for n in range(PIVOTS):
                    new = new - cols[n][g - first] * scaled[n]
                if g == first:
                    kept = rows[g]
                    for m in range(PIVOTS):
                        kept = jnp.where(sub == low + m, final[m], kept)
                    new = jnp.where(sub >= low + PIVOTS, new, kept)
                rows[g] = new
    return [
        jnp.concatenate([jnp.where(local <= 8 * g + sub, rows[g], 0.0) for g in range(8)], axis=0)
        for rows in groups
    ]

def beside(x, y):
    return jnp.concatenate([x, y], axis=1)

def paired(block):
    wide = jnp.concatenate([block, block], axis=0)
    row = lax.broadcasted_iota(jnp.int32, (128, 128), 0)
    col = lax.broadcasted_iota(jnp.int32, (128, 128), 1)
    return jnp.where((row // 64) == (col // 64), wide, 0.0)

def factor_kernel(
    gram_left, gram_right, tall_left, tall_right, out_left, out_right, s_ref, a_ref, y_ref, l_ref, w_ref
):
    owned = gram_left.shape[0]
    count = 2 * owned
    outs = [out_left.at[i] for i in range(owned)] + [out_right.at[i] for i in range(owned)]
    step = pl.program_id(0)

    @pl.when(step == 0)
    def _():
        s_ref[:owned] = gram_left[...]
        s_ref[owned:] = gram_right[...]
        a_ref[:owned] = tall_left[...]
        a_ref[owned:] = tall_right[...]

    start = pl.multiple_of(step * 128, 128)
    diag = [s_ref[i, pl.ds(start, 128), pl.ds(start, 128)] for i in range(count)]
    pairs = range(count // 2)
    top = pair_inverse([beside(diag[2 * p][:64, :64], diag[2 * p + 1][:64, :64]) for p in pairs])
    cross, below = [], []
    for p in pairs:
        low = beside(diag[2 * p][64:, :64], diag[2 * p + 1][64:, :64])
        factor = _nt(low, paired(top[p]))
        cross.append(factor)
        rest = beside(diag[2 * p][64:, 64:], diag[2 * p + 1][64:, 64:])
        below.append(rest - _nt(factor, paired(factor)))
    bottom = pair_inverse(below)
    for p in pairs:
        corner = -_nn(_nn(bottom[p], paired(cross[p])), paired(top[p]))
        zero = jnp.zeros((64, 64), jnp.float32)
        for side in range(2):
            cut = slice(64 * side, 64 * side + 64)
            w_ref[2 * p + side, :64] = beside(top[p][:, cut], zero)
            w_ref[2 * p + side, 64:] = beside(corner[:, cut], bottom[p][:, cut])

    @pl.when(step % 2 == 0)
    def _():
        for i in range(count):
            inv = w_ref[i]
            y_ref[i, :128, :128] = inv
            y_ref[i, :128, 128:] = jnp.zeros((128, 128), jnp.float32)
            low = s_ref[i, pl.ds(start + 128, 128), pl.ds(start, 128)]
            factor = _nt(low, inv)
            l_ref[i] = factor
            s_ref[i, pl.ds(start + 128, 128), pl.ds(start + 128, 128)] -= _nt(factor, factor)

    @pl.when(step % 2 == 1)
    def _():
        for i in range(count):
            inv = w_ref[i]
            y_ref[i, 128:, :128] = -_nn(_nn(inv, l_ref[i]), y_ref[i, :128, :128])
            y_ref[i, 128:, 128:] = inv

    @pl.when(step == 1)
    def _():
        for i in range(count):
            inv = y_ref[i]
            factor = _nt(s_ref[i, 256:, :256], inv)
            s_ref[i, 256:, 256:] -= _nt(factor, factor)
            inv = _split(inv)
            done = _three(NT, _split(a_ref[i, :, :256]), inv)
            outs[i][:, :256] = done
            a_ref[i, :, 256:] -= _three(NT, _split(done), _split(factor))

    @pl.when(step == 3)
    def _():
        for i in range(count):
            outs[i][:, 256:] = _three(NT, _split(a_ref[i, :, 256:]), _split(y_ref[i]))

def orthonormal_all(grams, talls):
    count = 2 * grams[0].shape[0]
    whole = lambda: pl.BlockSpec(memory_space=pltpu.VMEM)
    return pl.pallas_call(
        factor_kernel,
        grid=(4,),
        out_shape=[jax.ShapeDtypeStruct(tall.shape, jnp.float32) for tall in talls],
        in_specs=[whole() for _ in range(4)],
        out_specs=[whole(), whole()],
        scratch_shapes=[
            pltpu.VMEM((count, 512, 512), jnp.float32),
            pltpu.VMEM((count, 512, 512), jnp.float32),
            pltpu.VMEM((count, 256, 256), jnp.float32),
            pltpu.VMEM((count, 128, 128), jnp.float32),
            pltpu.VMEM((count, 128, 128), jnp.float32),
        ],
        name="orthonormal",
    )(*grams, *talls)


def high_dot(matrix_a, matrix_b, dims):
    return lax.dot_general(
        matrix_a, matrix_b, dims, precision=lax.Precision.HIGH, preferred_element_type=jnp.float32
    )


def low_dot(matrix_a, matrix_b, dims):
    return lax.dot_general(
        matrix_a.astype(jnp.bfloat16),
        matrix_b.astype(jnp.bfloat16),
        dims,
        preferred_element_type=jnp.float32,
    )


PLAIN = (((2,), (1,)), ((0,), (0,)))
FIRST = (((1,), (1,)), ((0,), (0,)))
SECOND = (((2,), (2,)), ((0,), (0,)))


def soap_update(
    weight,
    gradient,
    moment_one,
    moment_two,
    left_stats,
    right_stats,
    left_basis,
    right_basis,
    steps_done,
    rest,
):
    owned = weight.shape[0]
    turned = high_dot(left_basis, gradient.astype(jnp.float32), FIRST)
    rotated = high_dot(turned, right_basis, PLAIN)
    moment_one = beta_first * moment_one + (1.0 - beta_first) * rotated
    moment_two = beta_second * moment_two + (1.0 - beta_second) * rotated * rotated
    direction = (
        moment_one
        / (1.0 - beta_first**steps_done)
        / (jnp.sqrt(moment_two / (1.0 - beta_second**steps_done)) + epsilon)
    )
    direction = lax.optimization_barrier(direction.astype(jnp.bfloat16))
    weight = weight - learn_rate * (
        low_dot(low_dot(left_basis, direction, PLAIN), right_basis, SECOND) + decay_weight * weight
    )
    left_stats = beta_stats * left_stats + (1.0 - beta_stats) * low_dot(gradient, gradient, SECOND)
    right_stats = beta_stats * right_stats + (1.0 - beta_stats) * low_dot(gradient, gradient, FIRST)
    talls = (high_dot(left_stats, left_basis, PLAIN), high_dot(right_stats, right_basis, PLAIN))
    talls = advance(rest, talls)
    grams = tuple(high_dot(tall, tall, FIRST) for tall in talls)
    grams = advance(rest, grams)
    left_new, right_new = orthonormal_all(grams, talls)
    initial = high_dot(high_dot(left_basis, moment_one, PLAIN), right_basis, SECOND)
    moment_one = low_dot(low_dot(left_new, initial, FIRST), right_new, PLAIN)
    return (weight, moment_one, moment_two, left_stats, right_stats, left_new, right_new)


def swap(values, axis, bit):
    return lax.ppermute(values, axis, [(i, i ^ bit) for i in range(lax.axis_size(axis))])


def side_of(axis, bit):
    return (lax.axis_index(axis) // bit) % 2


def ordered(values, others, axis, bit, dim):
    first = side_of(axis, bit) == 0
    return jnp.concatenate(
        [jnp.where(first, values, others), jnp.where(first, others, values)], axis=dim
    )


def halves(values, axis, bit, dim):
    width = values.shape[dim] // 2
    side = side_of(axis, bit)
    return (
        lax.dynamic_slice_in_dim(values, side * width, width, dim),
        lax.dynamic_slice_in_dim(values, (1 - side) * width, width, dim),
    )


def bits_of(axis):
    count = lax.axis_size(axis)
    return [1 << i for i in range(count.bit_length() - 1)]


def scatter_half(values, axis, bit, dim):
    kept, sent = halves(values, axis, bit, dim)
    return kept + swap(sent, axis, bit)


def all_sum(values):
    for axis in ("opt", "tm"):
        for bit in bits_of(axis):
            values = values + swap(values, axis, bit)
    return values


def gather_blocks(values, axis, bits):
    for bit in bits:
        values = ordered(values, swap(values, axis, bit), axis, bit, 0)
    return values


ROWS = 256
DNT = (((1,), (1,)), ((), ()))
DTN = (((0,), (0,)), ((), ()))


def dot_as(dims, x, y):
    return lax.dot_general(x, y, dims, preferred_element_type=jnp.float32)


def fetch_taps(place_ref, sources, taps_ref, sem, layer):
    owned = sources[0].shape[0]
    for j in range(6):
        place = place_ref[6 * layer + j]
        for r, source in enumerate(sources):

            @pl.when(place // owned == r)
            def _(source=source):
                pltpu.make_async_copy(source.at[place % owned], taps_ref.at[j], sem.at[j]).start()


def await_taps(sources, taps_ref, sem):
    for j in range(6):
        pltpu.make_async_copy(sources[0].at[0], taps_ref.at[j], sem.at[j]).wait()


def sigmoid(x):
    return 0.5 * jnp.tanh(0.5 * x) + 0.5


def gate_inputs(
    layer, info_ref, cond_refs, weight_refs, aux_ref, crop_ref, crop, base, dilation, taps_ref
):
    sums = []
    for half in range(2):
        parts = []
        for block in range(2):
            spot = info_ref[NMAT + 4 * layer + 2 * half + block]
            part = dot_as(NN, cond_refs[0][...], weight_refs[0][spot])
            parts.append(part + dot_as(NN, cond_refs[1][...], weight_refs[1][spot]))
        total = jnp.concatenate(parts, axis=1) + aux_ref[4 + 2 * layer + half : 5 + 2 * layer + half, :]
        for k in range(3):
            window = crop_ref[crop, pl.ds(base + dilation * k, ROWS), :]
            total = total + dot_as(NN, window, taps_ref[2 * k + half])
        sums.append(total)
    return sums


def start_rows(mixed, aux_ref):
    total = mixed[:, 3:4] * aux_ref[3:4, :]
    for j in range(3):
        total = total + mixed[:, j : j + 1] * aux_ref[j : j + 1, :]
    return total


def first_kernel(
    place_ref, mixed_ref, aux_ref, cond_own, cond_other, rows_own, rows_other, out_own, out_other, w0, w1, w2, w3,
    before_ref, gated_ref, next_ref, start_ref, out_ref, taps_ref, sem,
):
    step = pl.program_id(0)
    sources = (w0, w1, w2, w3)
    per_crop = pl.num_programs(0) // mixed_ref.shape[0]
    margin = FIRST_DILATION

    @pl.when(step == 0)
    def _():
        fetch_taps(place_ref, sources, taps_ref, sem, 0)
        for crop in range(mixed_ref.shape[0]):
            start_ref[crop] = start_rows(mixed_ref[crop], aux_ref).astype(jnp.bfloat16)
        for core, piece in enumerate((out_own, out_other)):
            for across in range(2):
                column = pl.multiple_of(place_ref[NMAT + 8 + 2 * core + across] * 128, 128)
                for t in range(8):
                    spot = place_ref[NMAT + t]
                    for matrix in range(3):
                        out_ref[matrix, 64 * t : 64 * t + 64, pl.ds(column, 128)] = piece[
                            spot, across, matrix
                        ]
        await_taps(sources, taps_ref, sem)

    crop = step // per_crop
    base = pl.multiple_of((step % per_crop) * ROWS, ROWS)
    left, right = gate_inputs(
        0, place_ref, (cond_own, cond_other), (rows_own, rows_other), aux_ref, start_ref, crop, base, margin, taps_ref
    )
    before_ref[:, :H] = left
    before_ref[:, H:] = right
    gated = (jnp.tanh(left) * sigmoid(right)).astype(jnp.bfloat16)
    gated_ref[...] = gated
    hidden = start_rows(mixed_ref[crop, pl.ds(base + margin, ROWS), :], aux_ref)
    hidden = hidden + dot_as(NN, gated, out_ref[0]) + aux_ref[8:9, :]
    next_ref[...] = hidden.astype(jnp.bfloat16)


def second_kernel(
    place_ref, scale_ref, flow_ref, own_ref, before_halo, after_halo, aux_ref, cells_ref,
    cond_own, cond_other, rows_own, rows_other, gated_ref, out_ref, w0, w1, w2, w3,
    skip_ref, grads_ref, low_ref, mixed_ref, sums_ref, left_ref, right_ref, taps_ref, wide_ref, end_ref, sem,
):
    step = pl.program_id(0)
    sources = (w0, w1, w2, w3)
    crops, length = own_ref.shape[:2]
    margin = 2 * FIRST_DILATION

    @pl.when(step == 0)
    def _():
        fetch_taps(place_ref, sources, taps_ref, sem, 1)
        wide_ref[:, :margin] = before_halo[...]
        wide_ref[:, margin : margin + length] = own_ref[...]
        wide_ref[:, margin + length :] = after_halo[...]
        sums_ref[...] = jnp.zeros_like(sums_ref)
        end_ref[...] = jnp.zeros_like(end_ref)
        end_ref[0:6] = aux_ref[11:17, :]
        await_taps(sources, taps_ref, sem)

    per_crop = length // ROWS
    crop = step // per_crop
    base = pl.multiple_of((step % per_crop) * ROWS, ROWS)
    left, right = gate_inputs(
        1, place_ref, (cond_own, cond_other), (rows_own, rows_other), aux_ref, wide_ref, crop, base, margin, taps_ref
    )
    tangent, part = jnp.tanh(left), sigmoid(right)
    gated = (tangent * part).astype(jnp.bfloat16)
    skip_ref[...] = gated
    total = dot_as(NN, gated_ref[...], out_ref[1]) + dot_as(NN, gated, out_ref[2])
    total = total + (aux_ref[9:10, :] + aux_ref[10:11, :])
    halves_total = _split(total)
    outputs = _three(DNT, halves_total, _split(end_ref[...]))
    lane = lax.broadcasted_iota(jnp.int32, outputs.shape, 1)
    row_lane = lane[0:1]
    bias = jnp.zeros((1, 128), jnp.float32)
    for j in range(6):
        bias = jnp.where(row_lane == j, flow_ref[j, 6], bias)
    outputs = outputs + bias
    inside = lane < 3
    log_scale = jnp.where(inside, outputs, 0.0)
    growth = jnp.exp(log_scale)
    cells = cells_ref[crop, pl.ds(base + FIRST_DILATION, ROWS), :]
    upper = jnp.concatenate([cells, jnp.zeros((ROWS, 120), jnp.float32)], axis=1)
    upper = jnp.where(inside, pltpu.roll(upper, 124, axis=1), 0.0)
    z_upper = jnp.where(inside, growth * upper + pltpu.roll(outputs, 125, axis=1), 0.0)
    scale = scale_ref[0]
    grad_z = scale * z_upper
    grad_upper = grad_z * growth
    mixed_ref[...] = grad_upper[:, :8]
    grad_log = jnp.where(inside, grad_upper * upper - scale, 0.0)
    grad_outputs = grad_log + pltpu.roll(grad_z, 3, axis=1)
    grad_skip = grad_outputs[:, 0:1] * end_ref[0:1, :]
    for j in range(1, 6):
        grad_skip = grad_skip + grad_outputs[:, j : j + 1] * end_ref[j : j + 1, :]
    grad_skip = grad_skip.astype(jnp.bfloat16)
    grads_ref[...] = grad_skip
    grad_gated = dot_as(DNT, grad_skip, out_ref[2])
    grad_left = (grad_gated * (1.0 - tangent * tangent) * part).astype(jnp.bfloat16)
    grad_right = (grad_gated * tangent * part * (1.0 - part)).astype(jnp.bfloat16)
    low_ref[:, :H] = grad_left
    low_ref[:, H:] = grad_right

    @pl.when(base == 0)
    def _():
        total = dot_as(DNT, grad_left[:margin], taps_ref[0])
        total = total + dot_as(DNT, grad_right[:margin], taps_ref[1])
        left_ref[crop] = total.astype(jnp.bfloat16)

    @pl.when(base == length - ROWS)
    def _():
        total = dot_as(DNT, grad_left[ROWS - margin :], taps_ref[4])
        total = total + dot_as(DNT, grad_right[ROWS - margin :], taps_ref[5])
        right_ref[crop] = total.astype(jnp.bfloat16)

    sums_ref[0:8] += _three(DTN, _split(grad_outputs), halves_total)[0:8]
    sums_ref[8:9] += jnp.sum(grad_left.astype(jnp.float32), axis=0, keepdims=True)
    sums_ref[9:10] += jnp.sum(grad_right.astype(jnp.float32), axis=0, keepdims=True)
    sums_ref[10:11] += jnp.sum(grad_skip.astype(jnp.float32), axis=0, keepdims=True)
    sums_ref[11:12, :128] += jnp.sum(grad_outputs, axis=0, keepdims=True)
    sums_ref[12:13, :128] += jnp.sum(0.5 * z_upper * z_upper - log_scale, axis=0, keepdims=True)


def third_kernel(
    place_ref, own_ref, before_halo, after_halo, grads_ref, before_ref, out_ref, w0, w1, w2, w3,
    hidden_ref, residual_ref, low_ref, sums_ref, taps_ref, wide_ref, sem,
):
    step = pl.program_id(0)
    sources = (w0, w1, w2, w3)
    crops, length = own_ref.shape[:2]
    margin = 2 * FIRST_DILATION

    @pl.when(step == 0)
    def _():
        fetch_taps(place_ref, sources, taps_ref, sem, 1)
        wide_ref[:, :margin] = jnp.zeros((crops, margin, 2 * H), jnp.bfloat16)
        wide_ref[:, margin : margin + length] = own_ref[...]
        wide_ref[:, margin + length :] = jnp.zeros((crops, margin, 2 * H), jnp.bfloat16)
        sums_ref[...] = jnp.zeros_like(sums_ref)
        await_taps(sources, taps_ref, sem)

    per_crop = length // ROWS
    crop = step // per_crop
    base = pl.multiple_of((step % per_crop) * ROWS, ROWS)
    total = None
    for k in range(3):
        for half in range(2):
            window = wide_ref[crop, pl.ds(base + margin * (2 - k), ROWS), H * half : H * half + H]
            part = dot_as(DNT, window, taps_ref[2 * k + half])
            total = part if total is None else total + part
    hidden_ref[...] = total

    @pl.when(base == 0)
    def _():
        hidden_ref[:margin] += before_halo[crop].astype(jnp.float32)

    @pl.when(base == length - ROWS)
    def _():
        hidden_ref[ROWS - margin :] += after_halo[crop].astype(jnp.float32)

    total = hidden_ref[...]
    residual = total.astype(jnp.bfloat16)
    residual_ref[...] = residual
    grad_gated = dot_as(DNT, grads_ref[...], out_ref[1]) + dot_as(DNT, residual, out_ref[0])
    tangent, part = jnp.tanh(before_ref[:, :H]), sigmoid(before_ref[:, H:])
    grad_left = (grad_gated * (1.0 - tangent * tangent) * part).astype(jnp.bfloat16)
    grad_right = (grad_gated * tangent * part * (1.0 - part)).astype(jnp.bfloat16)
    low_ref[:, :H] = grad_left
    low_ref[:, H:] = grad_right
    sums_ref[0:1] += jnp.sum(residual.astype(jnp.float32), axis=0, keepdims=True)
    sums_ref[1:2] += jnp.sum(grad_left.astype(jnp.float32), axis=0, keepdims=True)
    sums_ref[2:3] += jnp.sum(grad_right.astype(jnp.float32), axis=0, keepdims=True)


def taps_kernel(place_ref, *refs, layer, pieces, owned):
    inputs, low_ref = refs[:pieces], refs[pieces]
    outs = refs[-3 - 2 * owned : -3]
    wide_ref, buffer_ref, sem = refs[-3:]
    crops, length = low_ref.shape[:2]
    margin = FIRST_DILATION * 2**layer
    offset = 0
    for piece in inputs:
        width = piece.shape[1]
        for crop in range(crops):
            wide_ref[crop, offset : offset + width] = piece[crop]
        offset += width
    for k in range(3):
        for half in range(2):
            j = 2 * k + half
            total = None
            for crop in range(crops):
                window = wide_ref[crop, margin * k : margin * k + length]
                part = dot_as(DTN, window, low_ref[crop, :, H * half : H * half + H])
                total = part if total is None else total + part
            buffer_ref[j] = total.astype(jnp.bfloat16)
            place = place_ref[6 * layer + j]
            relation = place // owned
            target = (relation // 2) * owned + place % owned
            for d, out_ref in enumerate(outs):

                @pl.when(target == d)
                def _(out_ref=out_ref):
                    pltpu.make_async_copy(buffer_ref.at[j], out_ref.at[relation % 2], sem.at[j]).start()

    for j in range(6):
        pltpu.make_async_copy(buffer_ref.at[j], outs[0].at[0], sem.at[j]).wait()


def start_kernel(
    place_ref, low_ref, above_ref, cells_ref, aux_ref, w0, w1, w2, w3,
    start_ref, lower_ref, taps_ref, wide_ref, end_ref, sem,
):
    crop = pl.program_id(0)
    sources = (w0, w1, w2, w3)
    length = low_ref.shape[1]
    margin = FIRST_DILATION

    @pl.when(crop == 0)
    def _():
        fetch_taps(place_ref, sources, taps_ref, sem, 0)
        start_ref[...] = jnp.zeros_like(start_ref)
        end_ref[...] = jnp.zeros_like(end_ref)
        end_ref[0:3] = aux_ref[0:3, :]
        await_taps(sources, taps_ref, sem)

    wide_ref[...] = jnp.zeros_like(wide_ref)
    wide_ref[margin : margin + length] = above_ref[...]
    for k in range(3):
        flowing = dot_as(DNT, low_ref[0, :, :H], taps_ref[2 * k])
        flowing = flowing + dot_as(DNT, low_ref[0, :, H:], taps_ref[2 * k + 1])
        wide_ref[margin * k : margin * k + length] += flowing
    pieces = _split(wide_ref[...])
    cells = cells_ref[crop]
    cells = jnp.concatenate([cells, jnp.zeros((cells.shape[0], 120), jnp.float32)], axis=1)
    start_ref[...] += _three(DTN, _split(cells), pieces)[0:8]
    lower_ref[0] = _three(DNT, pieces, _split(end_ref[...]))[:, :8]


def smem():
    return pl.BlockSpec(memory_space=pltpu.SMEM)


def vmem():
    return pl.BlockSpec(memory_space=pltpu.VMEM)


def anywhere():
    return pl.BlockSpec(memory_space=pl.ANY)


def by_rows(width):
    return pl.BlockSpec((ROWS, width), lambda i: (i, 0))


def fixed(shape, index):
    return pl.BlockSpec(shape, lambda i: index)


def shaped(shape, dtype=jnp.float32):
    return jax.ShapeDtypeStruct(shape, dtype)


def taps_gradient(place, pieces, low, layer, owned, targets=()):
    crops, length = low.shape[:2]
    width = sum(piece.shape[1] for piece in pieces)
    return pl.pallas_call(
        lambda *refs: taps_kernel(*refs, layer=layer, pieces=len(pieces), owned=owned),
        out_shape=[shaped((2, H, H), jnp.bfloat16)] * (2 * owned),
        in_specs=[smem()] + [vmem() for _ in pieces] + [vmem()] + [anywhere() for _ in targets],
        out_specs=[anywhere()] * (2 * owned),
        scratch_shapes=[
            pltpu.VMEM((crops, width, H), jnp.bfloat16),
            pltpu.VMEM((6, H, H), jnp.bfloat16),
            pltpu.SemaphoreType.DMA((6,)),
        ],
        input_output_aliases={len(pieces) + 2 + i: i for i in range(len(targets))},
        name=f"taps_gradient_{layer}",
    )(place, *pieces, low, *targets)


def halo(cells, width):
    count = lax.axis_size("tm")
    head, tail = cells[:, :width], cells[:, cells.shape[1] - width :]
    return (
        lax.ppermute(tail, "tm", [(i, i + 1) for i in range(count - 1)]),
        lax.ppermute(head, "tm", [(i + 1, i) for i in range(count - 1)]),
    )


def gather_relative(values, axis, bits):
    for bit in bits:
        values = jnp.concatenate([values, swap(values, axis, bit)], axis=0)
    return values


def reduced_slot(kept, sent):
    other = yield sent, "opt", 1
    sent, kept = kept[1] + other[1], kept[0] + other[0]
    other = yield sent, "opt", 2
    part = kept.astype(jnp.float32) + other.astype(jnp.float32)
    bits = bits_of("tm")
    for bit in bits[:-1]:
        kept, sent = halves(part, "tm", bit, 0)
        other = yield sent.astype(jnp.bfloat16), "tm", bit
        part = kept + other.astype(jnp.float32)
    part = part.astype(jnp.bfloat16)
    other = yield part, "tm", bits[-1]
    part = part + other
    for bit in reversed(bits[:-1]):
        other = yield part, "tm", bit
        part = ordered(part, other, "tm", bit, 0)
    return part


def swap_all(values, axis, bit):
    return jax.tree.map(lambda value: swap(value, axis, bit), values)


def lowest_half(values, bit, dim):
    shape = values.shape
    values = values.reshape(*shape[:dim], shape[dim] // 2, 2, *shape[dim + 1 :])
    kept, sent = halves(values, "tm", bit, dim + 1)
    shape = (*shape[:dim], shape[dim] // 2, *shape[dim + 1 :])
    return kept.reshape(shape), sent.reshape(shape)


def wide(values):
    return jax.tree.map(lambda value: value.astype(jnp.float32), values)


def narrow(values):
    return jax.tree.map(lambda value: value.astype(jnp.bfloat16), values)


def spread_rest(cond, out, small):
    other = yield (cond[1], out[1], small), "opt", 1
    cond = [mine + theirs for mine, theirs in zip(cond[0], wide(other[0]))]
    out, small = out[0] + wide(other[1]), small + other[2]
    width = cond[0].shape[0] // 2
    other = yield (narrow([part[width:] for part in cond]), narrow(out[1]), small), "opt", 2
    cond = [mine[:width] + theirs for mine, theirs in zip(cond, wide(other[0]))]
    out, small = out[0] + wide(other[1]), small + other[2]
    count = lax.axis_size("tm")
    cond = jnp.concatenate(cond, axis=1).reshape(width, count, -1)
    cond = jnp.swapaxes(cond, 0, 1)
    out = out.reshape(out.shape[0], count, -1, out.shape[2])
    for bit in bits_of("tm"):
        cond, sent = lowest_half(cond, bit, 0)
        out, sent_out = lowest_half(out, bit, 1)
        other = yield (narrow(sent), narrow(sent_out), small), "tm", bit
        cond, out, small = cond + wide(other[0]), out + wide(other[1]), small + other[2]
    return cond[0].T, out[:, 0], small


def reduce_slots(keep, send, work, follow, entry):
    owned = len(keep)
    chunks = [reduced_slot(kept, sent) for kept, sent in zip(keep, send)]
    requests = {i: next(chunk) for i, chunk in enumerate(chunks)}
    answers, ready, stage = {}, {}, {}
    done, results, latest, held = {}, [], (), None
    slot = 0
    while len(done) < owned:
        for i in [i for i in answers if ready[i] == slot]:
            try:
                requests[i] = chunks[i].send(answers.pop(i))
            except StopIteration as stop:
                done[i] = stop.value
                continue
            if i == owned and requests[i][1] == "tm":
                held = requests.pop(i)
        if slot == entry:
            chunks.append(follow(results + [latest]))
            requests[owned] = next(chunks[owned])
        active = sorted(requests)
        task, inputs = work.get(slot, (None, ()))
        values, inputs, latest = lax.optimization_barrier(
            (tuple(requests[i][0] for i in active), inputs, latest)
        )
        if slot - 1 in work:
            results.append(latest)
        for value, i in zip(values, active):
            answers[i] = swap_all(value, *requests[i][1:])
            stage[i] = stage.get(i, 0) + 1
            ready[i] = slot + 1
            if i < owned and stage[i] == 1:
                ready[i] = 1 if i == 0 else 2
            if i < owned and stage[i] == 2:
                ready[i] = 3 + i
        latest = () if task is None else task(*inputs)
        requests = {}
        slot += 1
    total = jnp.stack([done[i] for i in range(owned)])
    value, total = lax.optimization_barrier((held[0], total))
    return total, [chunks[owned], value, held[1:]]


def advance(rest, tied):
    chunk, value, where = rest
    answer, tied = lax.optimization_barrier((swap_all(value, *where), tied))
    try:
        rest[1], *rest[2:] = (lambda value, *where: (value, where))(*chunk.send(answer))
    except StopIteration as stop:
        rest[:] = [None, stop.value, None]
    return tied


def finish(rest):
    while rest[0] is not None:
        try:
            value, *where = rest[0].send(swap_all(rest[1], *rest[2]))
            rest[1:] = [value, where]
        except StopIteration as stop:
            rest[:] = [None, stop.value, None]
    return rest[1]


def adamw_update(weight, gradient, moment_one, moment_two, steps_done, rate_value):
    moment_one = beta_first * moment_one + (1.0 - beta_first) * gradient
    moment_two = beta_second * moment_two + (1.0 - beta_second) * gradient * gradient
    direction = (
        moment_one
        / (1.0 - beta_first**steps_done)
        / (jnp.sqrt(moment_two / (1.0 - beta_second**steps_done)) + epsilon)
    )
    weight = weight - rate_value * (direction + decay_weight * weight)
    return (weight, moment_one, moment_two)


def shards(
    wave,
    crop_offsets,
    squeeze_order,
    mel,
    mel_index,
    soap_slots,
    step_count,
    in_weight,
    soap_first,
    soap_second,
    left_stats,
    right_stats,
    left_basis,
    right_basis,
    cond_weight,
    cond_first,
    cond_second,
    out_weight,
    out_first,
    out_second,
    aux_params,
    aux_first,
    aux_second,
    flow_params,
    flow_first,
    flow_second,
):
    crops_current = wave.shape[0]
    row_count = crops_current * G_DEV
    tokens_all = row_count * lax.axis_size("tm") * lax.axis_size("opt")
    scale_final = 1.0 / (6.0 * tokens_all)
    scale_early = early_weight / (2.0 * tokens_all)
    steps_done = step_count[0].astype(jnp.float32)
    owned = in_weight.shape[0]
    rank = lax.axis_index("opt")
    own = in_weight.astype(jnp.bfloat16)
    cond_part = cond_weight.astype(jnp.bfloat16).T
    out_part = out_weight.astype(jnp.bfloat16)[None]
    own, cond_part, out_part = lax.optimization_barrier((own, cond_part, out_part))
    cond_across, out_across = swap(cond_part, "opt", 2), swap(out_part, "opt", 2)
    own, cond_part, cond_across, out_part, out_across, wave, mel_index = lax.optimization_barrier(
        (own, cond_part, cond_across, out_part, out_across, wave, mel_index)
    )
    tm_rank, tm_bits = lax.axis_index("tm"), bits_of("tm")[::-1]
    count_tm = lax.axis_size("tm")
    segments = [
        lax.dynamic_slice_in_dim(wave[crop, 0], crop_offsets[crop], 8 * G_DEV, 0).reshape(G_DEV, 8)
        for crop in range(crops_current)
    ]
    chosen = jnp.arange(8, dtype=jnp.int32)[:, None] == squeeze_order[None, :]
    squeezed = full_dot(jnp.concatenate(segments), chosen.astype(jnp.float32))
    squeezed = squeezed.reshape(crops_current, G_DEV, 8)
    flow_matrix = flow_params[:, :6]
    mixed = full_dot(squeezed.reshape(row_count, 8)[:, 2:], flow_matrix.T)
    lower_half, upper_half = mixed[:, :3], mixed[:, 3:]
    cells = jnp.concatenate(
        [
            lower_half,
            jnp.ones((row_count, 1), jnp.float32),
            upper_half,
            jnp.zeros((row_count, 1), jnp.float32),
        ],
        axis=1,
    ).reshape(crops_current, G_DEV, 8)
    edge = jnp.concatenate([cells, squeezed], axis=2)
    edge_before, edge_after = halo(edge, FIRST_DILATION)
    edge = jnp.concatenate([edge_before, edge, edge_after], axis=1)
    cells_wide, squeezed_wide = edge[..., :8], edge[..., 8:]

    slots = jnp.arange(NMAT, dtype=jnp.int32)
    slot_of = jnp.sum(
        jnp.where(soap_slots[None, :] == slots[:, None], slots[None, :], 0), axis=1
    ).astype(jnp.int32)
    relation = (slot_of // owned) ^ rank
    place = ((relation % 2) * 2 + relation // 2) * owned + slot_of % owned

    spots = jnp.zeros((count_tm,), jnp.int32)
    for index, bit in enumerate(tm_bits):
        distance = jnp.arange(count_tm, dtype=jnp.int32) ^ tm_rank
        spots = spots + ((distance // bit) % 2) * (1 << index)
    columns = rank ^ jnp.array([0, 2, 1, 3], jnp.int32)

    across = swap(own, "opt", 2)
    cond_part = jnp.concatenate([cond_part, cond_across], axis=0)[None]
    out_part = jnp.concatenate([out_part, out_across], axis=0)[None]
    own_core = swap(own, "opt", 1)
    across_core = swap(across, "opt", 1)
    sources = (own, across, own_core, across_core)
    cond_part = gather_relative(cond_part, "tm", tm_bits)
    out_part = gather_relative(out_part, "tm", tm_bits)
    if count_tm != 8:
        fold = count_tm // 8
        cond_part = jnp.take(cond_part, spots, axis=0)
        cond_part = cond_part.reshape(8, fold, *cond_part.shape[1:])
        cond_part = jnp.moveaxis(cond_part, 1, 2).reshape(8, cond_part.shape[2], -1)
        out_part = jnp.take(out_part, spots, axis=0)
        out_part = out_part.reshape(8, fold, *out_part.shape[1:])
        out_part = jnp.moveaxis(out_part, 1, 3).reshape(8, 2, 3, 64, -1)
        spots = jnp.arange(8, dtype=jnp.int32)
    place = jnp.concatenate([place, spots, columns])

    spot_of = jnp.arange(2 * 4 * FR_DEV, dtype=jnp.int32)
    quarter = (spot_of // FR_DEV) % 4
    sample = 2 * (rank ^ (spot_of // (4 * FR_DEV)) ^ (2 * (quarter // 2))) + quarter % 2
    spread = (jnp.arange(8, dtype=jnp.int32)[:, None] == sample[None, :]).astype(jnp.bfloat16)
    frames = half_dot(mel_index.reshape(row_count, 8).astype(jnp.bfloat16), spread)
    hits = (frames == (spot_of % FR_DEV).astype(jnp.float32)[None, :]).astype(jnp.bfloat16)
    hits = hits.reshape(crops_current, G_DEV, 2, 4 * FR_DEV)
    same = jnp.eye(4, dtype=jnp.bfloat16)
    frame_blocks = (same[None, :, None, :, None] * mel[:, None, :, None, :]).reshape(
        crops_current, 4 * FR_DEV, 4 * MEL
    )
    cond_rows = tuple(
        jnp.einsum(
            "cgk,ckm->cgm", hits[:, :, side], frame_blocks, preferred_element_type=jnp.float32
        )
        .astype(jnp.bfloat16)
        .reshape(row_count, 4 * MEL)
        for side in (0, 1)
    )
    cond_part, out_part, cond_rows, cells_wide, squeezed_wide, place = lax.optimization_barrier(
        (cond_part, out_part, cond_rows, cells_wide, squeezed_wide, place)
    )
    cond_other = swap(cond_part, "opt", 1)
    out_other = swap(out_part, "opt", 1)
    steps = row_count // ROWS
    taps_scratch = [pltpu.VMEM((6, H, H), jnp.bfloat16)]
    sems = [pltpu.SemaphoreType.DMA((6,))]
    half_cols = 4 * MEL
    wide_rows = G_DEV + 2 * FIRST_DILATION
    before_first, gated_first, hidden_low, start_low, out_full = pl.pallas_call(
        first_kernel,
        grid=(steps,),
        out_shape=[
            shaped((row_count, 2 * H)),
            shaped((row_count, H), jnp.bfloat16),
            shaped((row_count, H), jnp.bfloat16),
            shaped((crops_current, wide_rows, H), jnp.bfloat16),
            shaped((3, H, H), jnp.bfloat16),
        ],
        in_specs=[smem(), vmem(), vmem(), by_rows(half_cols), by_rows(half_cols)]
        + [vmem()] * 4
        + [anywhere()] * 4,
        out_specs=[by_rows(2 * H), by_rows(H), by_rows(H), vmem(), vmem()],
        scratch_shapes=taps_scratch + sems,
        name="first_layer",
    )(
        place,
        cells_wide,
        aux_params,
        *cond_rows,
        cond_part,
        cond_other,
        out_part,
        out_other,
        *sources,
    )

    hidden_low = hidden_low.reshape(crops_current, G_DEV, H)
    margin = 2 * FIRST_DILATION
    hidden_halo = halo(hidden_low, margin)
    gated_second, grad_skip, low_second, grad_upper, sums_second, to_left, to_right = pl.pallas_call(
        second_kernel,
        grid=(steps,),
        out_shape=[
            shaped((row_count, H), jnp.bfloat16),
            shaped((row_count, H), jnp.bfloat16),
            shaped((row_count, 2 * H), jnp.bfloat16),
            shaped((row_count, 8)),
            shaped((16, H)),
            shaped((crops_current, margin, H), jnp.bfloat16),
            shaped((crops_current, margin, H), jnp.bfloat16),
        ],
        in_specs=[smem(), smem(), smem(), vmem(), vmem(), vmem(), vmem(), vmem()]
        + [by_rows(half_cols)] * 2
        + [vmem()] * 2
        + [by_rows(H), vmem()]
        + [anywhere()] * 4,
        out_specs=[by_rows(H), by_rows(H), by_rows(2 * H), by_rows(8), vmem(), vmem(), vmem()],
        scratch_shapes=taps_scratch
        + [pltpu.VMEM((crops_current, G_DEV + 2 * margin, H), jnp.bfloat16)]
        + [pltpu.VMEM((128, H), jnp.float32)]
        + sems,
        name="second_layer",
    )(
        place,
        jnp.full((1,), scale_final, jnp.float32),
        flow_params,
        hidden_low,
        *hidden_halo,
        aux_params,
        cells_wide,
        *cond_rows,
        cond_part,
        cond_other,
        gated_first,
        out_full,
        *sources,
    )
    low_cells = low_second.reshape(crops_current, G_DEV, 2 * H)
    low_halo = (
        lax.ppermute(to_right, "tm", [(i, i + 1) for i in range(count_tm - 1)]),
        lax.ppermute(to_left, "tm", [(i + 1, i) for i in range(count_tm - 1)]),
    )
    grad_slots = taps_gradient(
        place, (hidden_halo[0], hidden_low, hidden_halo[1]), low_cells, 1, owned
    )
    grad_hidden, grad_residual, low_first, sums_first = pl.pallas_call(
        third_kernel,
        grid=(steps,),
        out_shape=[
            shaped((row_count, H)),
            shaped((row_count, H), jnp.bfloat16),
            shaped((row_count, 2 * H), jnp.bfloat16),
            shaped((8, H)),
        ],
        in_specs=[smem(), vmem(), vmem(), vmem(), by_rows(H), by_rows(2 * H), vmem()]
        + [anywhere()] * 4,
        out_specs=[by_rows(H), by_rows(H), by_rows(2 * H), vmem()],
        scratch_shapes=taps_scratch
        + [pltpu.VMEM((crops_current, G_DEV + 2 * margin, 2 * H), jnp.bfloat16)]
        + sems,
        name="first_gradient",
    )(place, low_cells, *low_halo, grad_skip, before_first, out_full, *sources)
    low_first_cells = low_first.reshape(crops_current, G_DEV, 2 * H)
    grad_slots = taps_gradient(place, (start_low,), low_first_cells, 0, owned, grad_slots)
    def start_work(low, above, cells):
        start, lower = pl.pallas_call(
            start_kernel,
            grid=(crops_current,),
            out_shape=[shaped((8, H)), shaped((crops_current, wide_rows, 8))],
            in_specs=[
                smem(),
                pl.BlockSpec((1, G_DEV, 2 * H), lambda i: (i, 0, 0)),
                pl.BlockSpec((G_DEV, H), lambda i: (i, 0)),
                vmem(),
                vmem(),
            ]
            + [anywhere()] * 4,
            out_specs=[vmem(), pl.BlockSpec((1, wide_rows, 8), lambda i: (i, 0, 0))],
            scratch_shapes=taps_scratch
            + [pltpu.VMEM((wide_rows, H), jnp.float32), pltpu.VMEM((128, H), jnp.float32)]
            + sems,
            name="start_gradient",
        )(place, low, above, cells, aux_params, *sources)
        return (start[:4], lower.reshape(-1, 8)[:, :3])

    def cond_work(own_rows, other_rows, first, second):
        return tuple(
            tuple(rows_dot(rows, low).astype(kind) for low in (first, second))
            for rows, kind in ((own_rows, jnp.float32), (other_rows, jnp.bfloat16))
        )

    def out_work(first, second, above, skip):
        pairs = ((first, above), (first, skip), (second, skip))
        grads = jnp.stack([rows_dot(*pair) for pair in pairs])
        return tuple(
            jnp.stack(
                [
                    lax.dynamic_slice_in_dim(grads, (rank ^ core ^ bit) * 128, 128, 2)
                    for bit in (0, 2)
                ]
            )
            for core in (0, 1)
        )

    def out_parts(*inputs):
        own, other = out_work(*inputs)
        return own, other.astype(jnp.bfloat16)

    def rest_of(results):
        (grad_start, grad_lower), grad_cond, grad_out = results
        final_part = jnp.sum(sums_second[12]) + 0.5 * jnp.sum(lower_half * lower_half)
        early_part = 0.5 * jnp.sum(squeezed[..., :2] * squeezed[..., :2])
        flow_lower = rows_dot(grad_lower, squeezed_wide.reshape(-1, 8)[:, 2:], highest)
        flow_lower = flow_lower + scale_final * rows_dot(
            lower_half, squeezed.reshape(-1, 8)[:, 2:], highest
        )
        flow_upper = rows_dot(grad_upper[:, :3], squeezed.reshape(-1, 8)[:, 2:], highest)
        grad_flow = jnp.concatenate(
            [jnp.concatenate([flow_lower, flow_upper], axis=0), sums_second[11, :6][:, None]], axis=1
        )
        grad_aux = jnp.concatenate(
            [
                grad_start,
                sums_first[1:3],
                sums_second[8:10],
                sums_first[0:1],
                sums_second[10:11],
                sums_second[10:11],
                sums_second[0:6],
            ],
            axis=0,
        )
        small = jnp.concatenate(
            [grad_aux.reshape(-1), grad_flow.reshape(-1), jnp.stack([final_part, early_part])]
        )
        small = jnp.pad(small, (0, -small.shape[0] % 1024)).reshape(-1, 128)
        return spread_rest(grad_cond, grad_out, small)

    grad_owned, rest = reduce_slots(
        grad_slots[:owned],
        grad_slots[owned:],
        {
            2: (start_work, (low_first_cells, grad_hidden, cells_wide)),
            3: (cond_work, (*cond_rows, low_first, low_second)),
            4: (out_parts, (gated_first, gated_second, grad_residual, grad_skip)),
        },
        rest_of,
        5,
    )
    grad_owned = grad_owned.astype(jnp.float32)
    (
        in_new,
        soap_first_new,
        soap_second_new,
        left_stats_new,
        right_stats_new,
        left_basis_new,
        right_basis_new,
    ) = soap_update(
        in_weight,
        grad_owned,
        soap_first,
        soap_second,
        left_stats,
        right_stats,
        left_basis,
        right_basis,
        steps_done,
        rest,
    )
    grad_cond, grad_out, small = finish(rest)
    small = small.reshape(-1)
    filled = aux_params.size + flow_params.size + 2
    grad_aux = small[: aux_params.size].reshape(aux_params.shape)
    grad_flow = small[aux_params.size : filled - 2].reshape(flow_params.shape)
    parts = small[filled - 2 : filled]
    factor = jnp.linalg.cholesky(full_dot(flow_matrix, flow_matrix.T))
    log_det = jnp.sum(jnp.log(jnp.diagonal(factor)))
    inverse_t = jax.scipy.linalg.cho_solve((factor, True), flow_matrix)
    grad_flow = grad_flow.at[:, :6].add(-inverse_t / 6.0)
    loss = parts[0] * scale_final + parts[1] * scale_early - log_det / 6.0
    cond_new, cond_first_new, cond_second_new = adamw_update(
        cond_weight, grad_cond, cond_first, cond_second, steps_done, learn_rate
    )
    out_new, out_first_new, out_second_new = adamw_update(
        out_weight, grad_out, out_first, out_second, steps_done, learn_rate
    )
    aux_new, aux_first_new, aux_second_new = adamw_update(
        aux_params, grad_aux, aux_first, aux_second, steps_done, aux_rate
    )
    flow_new, flow_first_new, flow_second_new = adamw_update(
        flow_params, grad_flow, flow_first, flow_second, steps_done, learn_rate
    )
    return (
        loss,
        in_new,
        soap_first_new,
        soap_second_new,
        left_stats_new,
        right_stats_new,
        left_basis_new,
        right_basis_new,
        cond_new,
        cond_first_new,
        cond_second_new,
        out_new,
        out_first_new,
        out_second_new,
        aux_new,
        aux_first_new,
        aux_second_new,
        flow_new,
        flow_first_new,
        flow_second_new,
    )


def solution(mesh):
    placed = (
        P("opt", "tm", None),
        P("opt"),
        P(),
        P("opt", "tm", None),
        P("opt", "tm", None),
        P(),
        P(),
        P("opt", None, None),
        P("opt", None, None),
        P("opt", None, None),
        P("opt", None, None),
        P("opt", None, None),
        P("opt", None, None),
        P("opt", None, None),
        P("tm", "opt"),
        P("tm", "opt"),
        P("tm", "opt"),
        P(None, "tm", "opt"),
        P(None, "tm", "opt"),
        P(None, "tm", "opt"),
        P(),
        P(),
        P(),
        P(),
        P(),
        P(),
    )
    return jax.shard_map(
        shards,
        mesh=mesh,
        in_specs=placed,
        out_specs=(
            P(),
            P("opt", None, None),
            P("opt", None, None),
            P("opt", None, None),
            P("opt", None, None),
            P("opt", None, None),
            P("opt", None, None),
            P("opt", None, None),
            P("tm", "opt"),
            P("tm", "opt"),
            P("tm", "opt"),
            P(None, "tm", "opt"),
            P(None, "tm", "opt"),
            P(None, "tm", "opt"),
            P(),
            P(),
            P(),
            P(),
            P(),
            P(),
        ),
        check_vma=False,
    )
```
